32 devices in a mesh: gx: 2 (over y), gy: 4 (over x, core), col: 4 (over z).
Axes of the slice: x: 2, y: 2, z: 4, core: 2. Of those that a mesh axis runs over, the one named last changes fastest.
Arguments:
- vol_pts: float32 [3, 65536], P(None, ('gx', 'gy')), may hold values from 0 to 1
- surf_pts: float32 [3, 65536], P(None, 'col'), may hold values from 0 to 1
- surf_coef: float32 [3, 65536], P(None, 'col'), may hold values from -4 to 4
- vol_tile: int32 [32, 1024], P(('gx', 'gy', 'col')), may hold values from 0 to 63, as said below
- slot: int32 [32, 1024], P(('gx', 'gy', 'col')), may hold values from 0 to 127
- wanted: int32 [32, 4, 32], P(('gx', 'gy', 'col')), may hold values from 0 to 127, as said below
- live: int32 [32], P(('gx', 'gy', 'col')), may hold values from 256 to 1024, as said below
Outputs:
- displacement: float32 [3, 65536], P(None, ('gx', 'gy', 'col'))
The draws below stay inside these ranges and needn't reach their ends.
Inputs may be any that keep to these rules, and one draw needn't show every extreme that they name: Within one device the pairs (vol_tile, slot) are distinct. `wanted`: the 32 tiles one device requests from one index of col are distinct. Only the first live[d] slots of device d are pairs; some device has all 1024 live.
All inputs are finite; a program needn't handle non-finite values.
Results may differ from the reference program's by a relative error of at most 0.0003.
Values sent between devices are 32-bit elements; how exact they have to be, the bound alone decides.
No kernel may reach another device: no remote copies, remote signals or barrier semaphores. Data moves between devices by JAX's collectives and lax.ppermute only.
A program may use at most 64 MiB of HBM per device.

```python
import jax
import jax.numpy as jnp
from jax import lax

TILE = 128
VT_DEV = 16
ST_DEV = 128
PAIRS_DEV = 1024
REQ = 32
VTG = 64
NV = 65536
NS = 65536
N_COL = 4
DEVICES = 32


def pair_draw(key):
    keys = jax.random.split(jax.random.fold_in(key, 7), DEVICES)
    total = VT_DEV * N_COL * N_COL * REQ
    picked = jax.vmap(lambda k: jax.random.permutation(k, total)[:PAIRS_DEV])(keys)
    return picked.astype(jnp.int32)


def draw_vol_tile(key, part):
    return pair_draw(key) // (N_COL * REQ)


def draw_slot(key, part):
    return pair_draw(key) % (N_COL * REQ)


def draw_wanted(key, part):
    keys = jax.random.split(jax.random.fold_in(key, 11), DEVICES * N_COL)
    picked = jax.vmap(lambda k: jax.random.permutation(k, ST_DEV)[:REQ])(keys)
    return picked.reshape(DEVICES, N_COL, REQ).astype(jnp.int32)


def draw_live(key, part):
    first, second = jax.random.split(jax.random.fold_in(key, 13))
    counts = jax.random.randint(first, (DEVICES,), PAIRS_DEV // 4, PAIRS_DEV + 1)
    fullest = jax.random.randint(second, (), 0, DEVICES)
    return counts.at[fullest].set(PAIRS_DEV).astype(jnp.int32)


def shard_levels(rng, shape, shards, low, largest):
    def one(axis_at, parts):
        draws = jax.random.uniform(jax.random.fold_in(jax.random.fold_in(rng, 6), axis_at), (parts,), jnp.float32, low / len(shards), largest / len(shards))
        return jnp.repeat(jnp.exp(draws), shape[axis_at] // parts).reshape((-1,) + (1,) * (len(shape) - axis_at - 1))

    level = one(*shards[0])
    for cut in shards[1:]:
        level = level * one(*cut)
    return level


def gaussian(own_key, dims, spread, reach, cuts=(), kind=jnp.bfloat16):
    factor_of = shard_levels(own_key, dims, cuts, -0.22, 0.18) if cuts else 1.0
    drawn = jax.random.normal(own_key, dims, jnp.float32) * spread * factor_of
    return jnp.minimum(jnp.maximum(drawn, -reach), reach).astype(kind)


def setup_inputs(seed: int = 0) -> dict:
    key_list = jax.random.split(jax.random.key(seed), 8)
    vol_pts = jnp.clip(1.0 * jax.random.uniform(key_list[0], (3, NV), jnp.float32) ** shard_levels(key_list[0], (3, NV), ((1, 8),), -0.2, 0.2), 0.0, 1.0)
    surf_pts = jnp.clip(1.0 * jax.random.uniform(key_list[1], (3, NS), jnp.float32) ** shard_levels(key_list[1], (3, NS), ((1, 4),), -0.2, 0.2), 0.0, 1.0)
    surf_coef = gaussian(key_list[2], (3, NS), 0.3, 4.0, ((1, 4),), jnp.float32)
    vol_tile = draw_vol_tile(jax.random.fold_in(key_list[7], 71), 0)
    slot = draw_slot(jax.random.fold_in(key_list[7], 71), 0)
    wanted = draw_wanted(jax.random.fold_in(key_list[7], 71), 0)
    live = draw_live(jax.random.fold_in(key_list[7], 71), 0)
    return dict(vol_pts=vol_pts, surf_pts=surf_pts, surf_coef=surf_coef, vol_tile=vol_tile, slot=slot, wanted=wanted, live=live)


def reference(vol_pts, surf_pts, surf_coef, vol_tile, slot, wanted, live):
    vol_tiles = vol_pts.reshape(3, -1, TILE).transpose(1, 0, 2)
    surf_tiles = jnp.concatenate([surf_pts, surf_coef], 0).reshape(6, -1, TILE).transpose(1, 0, 2)

    def one_device(totals, inputs):
        device, pair_vol, pair_slot, requested, live_count = inputs
        group = device // N_COL
        peer = pair_slot // REQ
        surf_index = (peer * ST_DEV + requested[peer, pair_slot % REQ]).astype(jnp.int32)
        vol_index = (group * VTG + pair_vol).astype(jnp.int32)
        points = vol_tiles[vol_index]
        sources = surf_tiles[surf_index]
        squared = jnp.zeros((PAIRS_DEV, TILE, TILE), jnp.float32)
        for comp in range(3):
            diff = points[:, comp, :, None] - sources[:, comp, None, :]
            squared = squared + diff * diff
        radius = jnp.sqrt(squared) / 1.2
        falloff = jnp.maximum(1.0 - radius, 0.0)
        kernel = falloff ** 4 * (4.0 * radius + 1.0)
        is_live = jnp.arange(PAIRS_DEV, dtype=jnp.int32) < live_count
        kernel = jnp.where(is_live[:, None, None], kernel, 0.0)
        motion = jnp.einsum('pij,pkj->pki', kernel, sources[:, 3:], precision=lax.Precision.HIGHEST)
        return (totals.at[vol_index].add(motion), None)
    start = jnp.zeros((vol_tiles.shape[0], 3, TILE), jnp.float32)
    devices = jnp.arange(DEVICES, dtype=jnp.int32)
    totals, _ = lax.scan(one_device, start, (devices, vol_tile, slot, wanted, live))
    return totals.transpose(1, 0, 2).reshape(3, -1)
```

```python
import functools

import jax
import jax.numpy as jnp
from jax import lax
from jax.experimental import pallas as pl
from jax.experimental.pallas import tpu as pltpu
from jax.sharding import PartitionSpec as P

TILE = 128
RADIUS = 1.2
FEATS = 32
UNROLL = 8
F32, BF16, I32 = jnp.float32, jnp.bfloat16, jnp.int32


def dot(a, b, contract=((1,), (0,))):
    return lax.dot_general(a, b, (contract, ((), ())), preferred_element_type=F32)


def iota(shape, axis):
    return lax.broadcasted_iota(I32, shape, axis)


def sort_kernel(n_col, n_local, live_ref, vol_ref, slot_ref, wanted_ref, msg_ref):
    rows = vol_ref.shape[0]
    slots = wanted_ref.shape[1]
    req = slots // n_col
    slot = slot_ref[...]
    vol = vol_ref[...].astype(F32)
    position = iota((rows, TILE), 0) * TILE + iota((rows, TILE), 1)
    key = jnp.where(position < live_ref[0], slot // req, n_col)
    keys = n_col + 1
    keys += keys % 2
    masks = [(key == k).astype(F32) for k in range(keys)]
    mask = jnp.concatenate(masks, 0).astype(BF16)
    ahead = (iota((TILE, TILE), 0) < iota((TILE, TILE), 1)).astype(F32).astype(BF16)
    within = dot(mask, ahead)
    count = dot(mask, jnp.ones((TILE, TILE), BF16)).astype(BF16)
    total = keys * rows
    above = (iota((total, total), 1) < iota((total, total), 0)).astype(F32).astype(BF16)
    start = dot(above, count)
    rank = within + start
    dest = masks[0] * rank[:rows]
    for k in range(1, keys):
        dest += masks[k] * rank[k * rows : (k + 1) * rows]
    dest = dest.astype(I32)
    dest_row, dest_lane = dest // TILE, dest % TILE
    table = jnp.broadcast_to(wanted_ref[...], (8, slots)).astype(F32).astype(BF16)
    out = jnp.zeros((2 * rows, TILE), F32)
    for r in range(rows):
        row = slice(r, r + 1)
        chosen = (iota((slots, TILE), 0) == slot[row]).astype(F32).astype(BF16)
        tile = dot(table, chosen)[:1]
        here = (iota((rows, TILE), 0) == dest_row[row]).astype(F32)
        values = jnp.concatenate([here * vol[row], here * tile], 0).astype(BF16)
        lanes = (iota((TILE, TILE), 0) == dest_lane[row]).astype(F32).astype(BF16)
        out += dot(values, lanes, ((1,), (1,)))
    out = out.astype(I32)
    msg_ref[:rows] = out[:rows] * n_local + out[rows:]
    tail = jnp.concatenate([start[k * rows : k * rows + 1] for k in range(keys)], 0)
    pad = msg_ref.shape[0] - rows - keys
    if pad:
        tail = jnp.concatenate([tail, jnp.zeros((pad, TILE), F32)], 0)
    msg_ref[rows:] = tail.astype(I32)


def thirds(a):
    one = a.astype(BF16).astype(F32)
    two = (a - one).astype(BF16).astype(F32)
    return one, two, a - one - two


def point_features(points):
    a = (points - 0.5) * (1.0 / RADIUS)
    norm = a[0:1] * a[0:1] + a[1:2] * a[1:2] + a[2:3] * a[2:3]
    return thirds(a), jnp.concatenate(thirds(norm), 0)


def main_kernel(
    n_col, n_local, list_rows, me_ref, *refs
):
    msgs = refs[:n_col]
    vol_ref, pts_ref, coef_ref = refs[n_col : n_col + 3]
    outs = refs[n_col + 3 : 2 * n_col + 3]
    lists, flat, surf, vols, coefs, acc, dist, kern, sems = refs[2 * n_col + 3 :]
    msg_rows = msgs[0].shape[0]
    copies = [
        pltpu.make_async_copy(msgs[k], lists.at[pl.ds(k * msg_rows, msg_rows)], sems.at[k])
        for k in range(n_col)
    ]
    for c in copies:
        c.start()
    acc[...] = jnp.zeros_like(acc)

    group_tiles = vols.shape[0]
    step = 8
    ones = jnp.ones((3, step * TILE), F32)
    blank = jnp.zeros((FEATS - 24, step * TILE), F32)

    def surface(b, _):
        lanes = pl.ds(pl.multiple_of(b * step * TILE, step * TILE), step * TILE)
        (one, two, three), norm = point_features(pts_ref[:, lanes])
        one, two, three = -2.0 * one, -2.0 * two, -2.0 * three
        rows = jnp.concatenate([one, two, one, three, one, two, norm, ones, blank], 0)
        coef = coef_ref[:, lanes] * 4.0
        high = coef.astype(BF16).astype(F32)
        pair = jnp.concatenate([high, coef - high, jnp.zeros((2, step * TILE), F32)], 0)
        for t in range(step):
            span = slice(t * TILE, (t + 1) * TILE)
            surf[b * step + t] = rows[:, span].T.astype(BF16)
            tile = pair[:, span].astype(BF16)
            coefs[b * step + t] = jnp.concatenate([tile, tile], 1)
        return 0

    lax.fori_loop(0, n_local // step, surface, 0)
    surf[n_local] = jnp.zeros((TILE, FEATS), BF16)
    coefs[n_local] = jnp.zeros((8, 2 * TILE), BF16)

    def volume(b, _):
        lanes = pl.ds(pl.multiple_of(b * step * TILE, step * TILE), step * TILE)
        (one, two, three), norm = point_features(vol_ref[:, lanes])
        rows = jnp.concatenate([one, one, two, one, three, two, ones, norm, blank], 0).astype(BF16)
        for t in range(step):
            vols[b * step + t] = rows[:, t * TILE : (t + 1) * TILE]
        return 0

    lax.fori_loop(0, group_tiles // step, volume, 0)

    for c in copies:
        c.wait()
    me = me_ref[0]
    ends, shifts = [], []
    total = jnp.int32(0)
    for k in range(n_col):
        first = lists[k * msg_rows + list_rows + me, 0]
        last = lists[k * msg_rows + list_rows + me + 1, 0]
        shifts.append(k * msg_rows * TILE + first - total)
        total = total + (last - first)
        ends.append(total)

    def fetch(p):
        shift = shifts[0]
        for k in range(1, n_col):
            shift = jnp.where(p >= ends[k - 1], shifts[k], shift)
        valid = p < total
        at = jnp.where(valid, p + shift, 0)
        pair = lists[at // TILE, at % TILE]
        pair = jnp.where(valid, pair, -1)
        flat[p] = pair
        return pair

    def parts(pair):
        valid = pair >= 0
        return (
            jnp.where(valid, pair // n_local, 0),
            jnp.where(valid, pair % n_local, n_local),
        )

    def distances(b, slot):
        for q in range(UNROLL):
            v, s = parts(fetch(b * UNROLL + q))
            dist[slot, q] = dot(surf[s], vols[v])

    def kernels(slot):
        for q in range(UNROLL):
            squared = jnp.minimum(jnp.maximum(dist[slot, q], 1e-12), 1.0)
            radius = squared * lax.rsqrt(squared)
            falloff = 1.0 - radius
            falloff = falloff * falloff
            value = falloff * falloff * (radius + 0.25)
            high = value.astype(BF16)
            kern[slot, q, :TILE] = high
            kern[slot, q, TILE:] = (value - high.astype(F32)).astype(BF16)

    def motions(b, slot):
        for q in range(UNROLL):
            v, s = parts(flat[b * UNROLL + q])
            acc[v] += dot(coefs[s], kern[slot, q])

    trips = jnp.maximum((total + 2 * UNROLL - 1) // (2 * UNROLL), 1)
    distances(0, 0)
    kernels(0)
    distances(1, 1)

    def trip(h, _):
        b = 2 * h
        motions(b - 2, 0)
        kernels(1)
        distances(b, 0)
        motions(b - 1, 1)
        kernels(0)
        distances(b + 1, 1)
        return 0

    lax.fori_loop(1, trips, trip, 0)
    b = 2 * trips
    motions(b - 2, 0)
    kernels(1)
    motions(b - 1, 1)

    share = group_tiles // n_col
    for k in range(n_col):
        base = lax.rem(me + k, n_col) * share
        for t in range(share):
            value = acc[base + t]
            outs[k][:, t * TILE : (t + 1) * TILE] = value[:3] + value[3:6]


def shift_right(x, k, n):
    return lax.ppermute(x, "col", [(i, (i + k) % n) for i in range(n)])


def per_device(vol_pts, surf_pts, surf_coef, vol_tile, slot, wanted, live):
    n_col = lax.axis_size("col")
    me = lax.axis_index("col").astype(I32).reshape(1)
    n_local = surf_pts.shape[1] // TILE
    group_tiles = vol_pts.shape[1] // TILE
    share = group_tiles // n_col
    list_rows = vol_tile.shape[1] // TILE
    msg_rows = -(-(list_rows + n_col + 2) // 8) * 8
    smem = pl.BlockSpec(memory_space=pltpu.SMEM)
    vmem = pl.BlockSpec(memory_space=pltpu.VMEM)
    msg = pl.pallas_call(
        functools.partial(sort_kernel, n_col, n_local),
        out_shape=jax.ShapeDtypeStruct((msg_rows, TILE), I32),
        in_specs=[smem, vmem, vmem, vmem],
        out_specs=vmem,
        name="sort_pairs",
    )(live, vol_tile.reshape(-1, TILE), slot.reshape(-1, TILE), wanted.reshape(1, -1))
    msgs = [msg] + [shift_right(msg, k, n_col) for k in range(1, n_col)]
    room = n_col * list_rows * TILE + 4 * UNROLL
    parts = pl.pallas_call(
        functools.partial(main_kernel, n_col, n_local, list_rows),
        out_shape=[jax.ShapeDtypeStruct((3, share * TILE), F32)] * n_col,
        in_specs=[smem] + [pl.BlockSpec(memory_space=pl.ANY)] * n_col + [vmem] * 3,
        out_specs=[vmem] * n_col,
        scratch_shapes=[
            pltpu.SMEM((n_col * msg_rows, TILE), I32),
            pltpu.SMEM((room,), I32),
            pltpu.VMEM((n_local + 1, TILE, FEATS), BF16),
            pltpu.VMEM((group_tiles, FEATS, TILE), BF16),
            pltpu.VMEM((n_local + 1, 8, 2 * TILE), BF16),
            pltpu.VMEM((group_tiles, 8, TILE), F32),
            pltpu.VMEM((2, UNROLL, TILE, TILE), F32),
            pltpu.VMEM((2, UNROLL, 2 * TILE, TILE), BF16),
            pltpu.SemaphoreType.DMA((n_col,)),
        ],
        compiler_params=pltpu.CompilerParams(vmem_limit_bytes=48 << 20),
        name="pair_sums",
    )(me, *msgs, vol_pts, surf_pts, surf_coef)
    out = parts[0]
    for k in range(1, n_col):
        out = out + shift_right(parts[k], k, n_col)
    return out


def solution(mesh):
    return jax.shard_map(
        per_device,
        mesh=mesh,
        in_specs=(
            P(None, ("gx", "gy")),
            P(None, "col"),
            P(None, "col"),
            P(("gx", "gy", "col"), None),
            P(("gx", "gy", "col"), None),
            P(("gx", "gy", "col"), None, None),
            P(("gx", "gy", "col")),
        ),
        out_specs=P(None, ("gx", "gy", "col")),
        check_vma=False,
    )
```

```python
import functools

import jax
import jax.numpy as jnp
from jax import lax
from jax.experimental import pallas as pl
from jax.experimental.pallas import tpu as pltpu
from jax.sharding import PartitionSpec as P

TILE = 128
RADIUS = 1.2
FEATS = 32
UNROLL = 32
F32, BF16, I32 = jnp.float32, jnp.bfloat16, jnp.int32


def dot(a, b, contract=((1,), (0,))):
    return lax.dot_general(a, b, (contract, ((), ())), preferred_element_type=F32)


def iota(shape, axis):
    return lax.broadcasted_iota(I32, shape, axis)


def sort_kernel(n_col, n_local, live_ref, vol_ref, slot_ref, wanted_ref, msg_ref):
    rows = vol_ref.shape[0]
    req = wanted_ref.shape[2]
    slot = slot_ref[...]
    vol = vol_ref[...].astype(F32)
    position = iota((rows, TILE), 0) * TILE + iota((rows, TILE), 1)
    key = jnp.where(position < live_ref[0], slot // req, n_col)
    keys = n_col + 1
    keys += keys % 2
    masks = [(key == k).astype(F32) for k in range(keys)]
    mask = jnp.concatenate(masks, 0).astype(BF16)
    ahead = (iota((TILE, TILE), 0) < iota((TILE, TILE), 1)).astype(F32).astype(BF16)
    within = dot(mask, ahead)
    count = dot(mask, jnp.ones((TILE, TILE), BF16)).astype(BF16)
    total = keys * rows
    above = (iota((total, total), 1) < iota((total, total), 0)).astype(F32).astype(BF16)
    start = dot(above, count)
    rank = within + start
    dest = masks[0] * rank[:rows]
    for k in range(1, keys):
        dest += masks[k] * rank[k * rows : (k + 1) * rows]
    dest = dest.astype(I32)
    dest_row, dest_lane = dest // TILE, dest % TILE
    table = wanted_ref[0].astype(F32)
    if n_col % 8:
        table = jnp.concatenate([table, jnp.zeros((8 - n_col % 8, req), F32)], 0)
    table = table.astype(BF16)
    peer, place = slot // req, slot % req
    out = jnp.zeros((2 * rows, TILE), F32)
    for r in range(rows):
        row = slice(r, r + 1)
        chosen = (iota((req, TILE), 0) == place[row]).astype(F32).astype(BF16)
        tiles = dot(table, chosen)
        tiles = jnp.where(iota(tiles.shape, 0) == peer[row], tiles, 0.0)
        tile = jnp.sum(tiles, 0, keepdims=True)
        here = (iota((rows, TILE), 0) == dest_row[row]).astype(F32)
        values = jnp.concatenate([here * vol[row], here * tile], 0).astype(BF16)
        lanes = (iota((TILE, TILE), 0) == dest_lane[row]).astype(F32).astype(BF16)
        out += dot(values, lanes, ((1,), (1,)))
    out = out.astype(I32)
    msg_ref[:rows] = out[:rows] * n_local + out[rows:]
    tail = jnp.concatenate([start[k * rows : k * rows + 1] for k in range(keys)], 0)
    pad = msg_ref.shape[0] - rows - keys
    if pad:
        tail = jnp.concatenate([tail, jnp.zeros((pad, TILE), F32)], 0)
    msg_ref[rows:] = tail.astype(I32)


def thirds(a):
    one = a.astype(BF16).astype(F32)
    two = (a - one).astype(BF16).astype(F32)
    return one, two, a - one - two


def point_features(points):
    a = (points - 0.5) * (1.0 / RADIUS)
    norm = a[0:1] * a[0:1] + a[1:2] * a[1:2] + a[2:3] * a[2:3]
    return thirds(a), jnp.concatenate(thirds(norm), 0)


def feature_kernel(vol_ref, pts_ref, coef_ref, surf, vols, coefs):
    n_local, group_tiles = surf.shape[0] - 1, vols.shape[0]
    step = 8
    ones = jnp.ones((3, step * TILE), F32)
    blank = jnp.zeros((FEATS - 24, step * TILE), F32)

    def surface(b, _):
        lanes = pl.ds(pl.multiple_of(b * step * TILE, step * TILE), step * TILE)
        (one, two, three), norm = point_features(pts_ref[:, lanes])
        one, two, three = -2.0 * one, -2.0 * two, -2.0 * three
        rows = jnp.concatenate([one, two, one, three, one, two, norm, ones, blank], 0)
        coef = coef_ref[:, lanes] * 4.0
        high = coef.astype(BF16).astype(F32)
        pair = jnp.concatenate([high, coef - high, jnp.zeros((2, step * TILE), F32)], 0)
        for t in range(step):
            span = slice(t * TILE, (t + 1) * TILE)
            surf[b * step + t] = rows[:, span].T.astype(BF16)
            tile = pair[:, span].astype(BF16)
            coefs[b * step + t] = jnp.concatenate([tile, tile], 1)
        return 0

    lax.fori_loop(0, n_local // step, surface, 0)
    surf[n_local] = jnp.zeros((TILE, FEATS), BF16)
    coefs[n_local] = jnp.zeros((8, 2 * TILE), BF16)

    def volume(b, _):
        lanes = pl.ds(pl.multiple_of(b * step * TILE, step * TILE), step * TILE)
        (one, two, three), norm = point_features(vol_ref[:, lanes])
        rows = jnp.concatenate([one, one, two, one, three, two, ones, norm, blank], 0).astype(BF16)
        for t in range(step):
            vols[b * step + t] = rows[:, t * TILE : (t + 1) * TILE]
        return 0

    lax.fori_loop(0, group_tiles // step, volume, 0)


def main_kernel(n_col, n_local, list_rows, me_ref, *refs):
    msgs = refs[:n_col]
    surf, vols, coefs = refs[n_col : n_col + 3]
    outs = refs[n_col + 3 : 2 * n_col + 3]
    lists, flat, acc, kern, sems = refs[2 * n_col + 3 :]
    msg_rows = msgs[0].shape[0]
    copies = [
        pltpu.make_async_copy(msgs[k], lists.at[pl.ds(k * msg_rows, msg_rows)], sems.at[k])
        for k in range(n_col)
    ]
    for c in copies:
        c.start()
    acc[...] = jnp.zeros_like(acc)
    kern[...] = jnp.zeros_like(kern)
    for q in range(UNROLL):
        flat[q] = n_local
    group_tiles = vols.shape[0]
    bits = (n_local - 1).bit_length()
    for c in copies:
        c.wait()
    me = me_ref[0]
    ends, shifts = [], []
    total = jnp.int32(0)
    for k in range(n_col):
        first = lists[k * msg_rows + list_rows + me, 0]
        last = lists[k * msg_rows + list_rows + me + 1, 0]
        shifts.append(k * msg_rows * TILE + first - total)
        total = total + (last - first)
        ends.append(total)

    def fetch(p):
        shift = shifts[0]
        for k in range(1, n_col):
            shift = jnp.where(p >= ends[k - 1], shifts[k], shift)
        valid = p < total
        at = jnp.where(valid, p + shift, 0)
        pair = lists[at >> 7, at & (TILE - 1)]
        v, s = pair >> bits, pair & ((1 << bits) - 1)
        v, s = jnp.where(valid, v, 0), jnp.where(valid, s, n_local)
        flat[p + UNROLL] = (v << (bits + 1)) | s
        return v, s

    def move(p, q):
        pair = flat[p]
        v, s = pair >> (bits + 1), pair & ((2 << bits) - 1)
        acc[v] += dot(coefs[s], kern[q])

    def evaluate(p, q):
        v, s = fetch(p)
        squared = dot(surf[s], vols[v])
        squared = jnp.minimum(jnp.maximum(squared, 1e-12), 1.0)
        radius = squared * lax.rsqrt(squared)
        falloff = 1.0 - radius
        falloff = falloff * falloff
        value = falloff * falloff * (radius + 0.25)
        high = value.astype(BF16)
        kern[q, :TILE] = high
        kern[q, TILE:] = (value - high.astype(F32)).astype(BF16)

    trips = (total + UNROLL - 1) // UNROLL

    def trip(h, _):
        for q in range(UNROLL):
            move(h * UNROLL + q, q)
            evaluate(h * UNROLL + q, q)
        return 0

    lax.fori_loop(0, trips, trip, 0)
    for q in range(UNROLL):
        move(trips * UNROLL + q, q)

    share = group_tiles // n_col
    for k in range(n_col):
        base = lax.rem(me + k, n_col) * share
        for t in range(share):
            value = acc[base + t]
            outs[k][:, t * TILE : (t + 1) * TILE] = value[:3] + value[3:6]


def shift_right(x, k, n):
    return lax.ppermute(x, "col", [(i, (i + k) % n) for i in range(n)])


def per_device(vol_pts, surf_pts, surf_coef, vol_tile, slot, wanted, live):
    n_col = lax.axis_size("col")
    me = lax.axis_index("col").astype(I32).reshape(1)
    n_local = surf_pts.shape[1] // TILE
    group_tiles = vol_pts.shape[1] // TILE
    share = group_tiles // n_col
    list_rows = vol_tile.shape[1] // TILE
    msg_rows = -(-(list_rows + n_col + 2) // 8) * 8
    smem = pl.BlockSpec(memory_space=pltpu.SMEM)
    vmem = pl.BlockSpec(memory_space=pltpu.VMEM)
    msg = pl.pallas_call(
        functools.partial(sort_kernel, n_col, n_local),
        out_shape=jax.ShapeDtypeStruct((msg_rows, TILE), I32),
        in_specs=[smem, vmem, vmem, vmem],
        out_specs=vmem,
        compiler_params=pltpu.CompilerParams(vmem_limit_bytes=8 << 20),
        name="sort_pairs",
    )(live, vol_tile.reshape(-1, TILE), slot.reshape(-1, TILE), wanted)
    msgs = [msg] + [shift_right(msg, k, n_col) for k in range(1, n_col)]
    room = n_col * list_rows * TILE + 4 * UNROLL
    features = pl.pallas_call(
        feature_kernel,
        out_shape=[
            jax.ShapeDtypeStruct((n_local + 1, TILE, FEATS), BF16),
            jax.ShapeDtypeStruct((group_tiles, FEATS, TILE), BF16),
            jax.ShapeDtypeStruct((n_local + 1, 8, 2 * TILE), BF16),
        ],
        in_specs=[vmem] * 3,
        out_specs=[vmem] * 3,
        compiler_params=pltpu.CompilerParams(vmem_limit_bytes=16 << 20),
        name="features",
    )(vol_pts, surf_pts, surf_coef)
    parts = pl.pallas_call(
        functools.partial(main_kernel, n_col, n_local, list_rows),
        out_shape=[jax.ShapeDtypeStruct((3, share * TILE), F32)] * n_col,
        in_specs=[smem] + [vmem] * (n_col + 3),
        out_specs=[vmem] * n_col,
        scratch_shapes=[
            pltpu.SMEM((n_col * msg_rows, TILE), I32),
            pltpu.SMEM((room,), I32),
            pltpu.VMEM((group_tiles, 8, TILE), F32),
            pltpu.VMEM((UNROLL, 2 * TILE, TILE), BF16),
            pltpu.SemaphoreType.DMA((n_col,)),
        ],
        compiler_params=pltpu.CompilerParams(vmem_limit_bytes=32 << 20),
        name="pair_sums",
    )(me, *msgs, *features)
    out = parts[0]
    for k in range(1, n_col):
        out = out + shift_right(parts[k], k, n_col)
    return out


def solution(mesh):
    return jax.shard_map(
        per_device,
        mesh=mesh,
        in_specs=(
            P(None, ("gx", "gy")),
            P(None, "col"),
            P(None, "col"),
            P(("gx", "gy", "col"), None),
            P(("gx", "gy", "col"), None),
            P(("gx", "gy", "col"), None, None),
            P(("gx", "gy", "col")),
        ),
        out_specs=P(None, ("gx", "gy", "col")),
        check_vma=False,
    )
```

```python
import functools

import jax
import jax.numpy as jnp
from jax import lax
from jax.experimental import pallas as pl
from jax.experimental.pallas import tpu as pltpu
from jax.sharding import PartitionSpec as P

TILE = 128
RADIUS = 1.2
FEATS = 32
UNROLL = 32
F32, BF16, I32 = jnp.float32, jnp.bfloat16, jnp.int32


def dot(a, b, contract=((1,), (0,))):
    return lax.dot_general(a, b, (contract, ((), ())), preferred_element_type=F32)


def tile_bits(n_local):
    return n_local.bit_length()


def iota(shape, axis):
    return lax.broadcasted_iota(I32, shape, axis)


def start_all(sems, *pairs):
    copies = [pltpu.make_async_copy(a, b, sems.at[k]) for k, (a, b) in enumerate(pairs)]
    for c in copies:
        c.start()
    return copies


def fetch_all(sems, *pairs):
    for c in start_all(sems, *pairs):
        c.wait()


def sort_kernel(n_col, n_local, live_ref, vol_hbm, slot_hbm, wanted_hbm, msg_ref, vol_ref, slot_ref, wanted_ref, sems):
    fetch_all(sems, (vol_hbm, vol_ref), (slot_hbm, slot_ref), (wanted_hbm, wanted_ref))
    rows = vol_ref.shape[0]
    req = wanted_ref.shape[2]
    slot = slot_ref[...]
    vol = vol_ref[...].astype(F32)
    position = iota((rows, TILE), 0) * TILE + iota((rows, TILE), 1)
    key = jnp.where(position < live_ref[0], slot // req, n_col)
    keys = n_col + 1
    keys += keys % 2
    masks = [(key == k).astype(F32) for k in range(keys)]
    mask = jnp.concatenate(masks, 0).astype(BF16)
    ahead = (iota((TILE, TILE), 0) < iota((TILE, TILE), 1)).astype(F32).astype(BF16)
    within = dot(mask, ahead)
    count = dot(mask, jnp.ones((TILE, TILE), BF16)).astype(BF16)
    total = keys * rows
    above = (iota((total, total), 1) < iota((total, total), 0)).astype(F32).astype(BF16)
    start = dot(above, count)
    rank = within + start
    dest = masks[0] * rank[:rows]
    for k in range(1, keys):
        dest += masks[k] * rank[k * rows : (k + 1) * rows]
    dest = dest.astype(I32)
    dest_row, dest_lane = dest // TILE, dest % TILE
    table = wanted_ref[0].astype(F32)
    if n_col % 8:
        table = jnp.concatenate([table, jnp.zeros((8 - n_col % 8, req), F32)], 0)
    table = table.astype(BF16)
    peer, place = slot // req, slot % req
    out = jnp.zeros((2 * rows, TILE), F32)
    for r in range(rows):
        row = slice(r, r + 1)
        chosen = (iota((req, TILE), 0) == place[row]).astype(F32).astype(BF16)
        tiles = dot(table, chosen)
        tiles = jnp.where(iota(tiles.shape, 0) == peer[row], tiles, 0.0)
        tile = jnp.sum(tiles, 0, keepdims=True)
        here = (iota((rows, TILE), 0) == dest_row[row]).astype(F32)
        values = jnp.concatenate([here * vol[row], here * tile], 0).astype(BF16)
        lanes = (iota((TILE, TILE), 0) == dest_lane[row]).astype(F32).astype(BF16)
        out += dot(values, lanes, ((1,), (1,)))
    out = out.astype(I32)
    msg_ref[:rows] = (out[:rows] << tile_bits(n_local)) | out[rows:]
    tail = jnp.concatenate([start[k * rows : k * rows + 1] for k in range(keys)], 0)
    pad = msg_ref.shape[0] - rows - keys
    if pad:
        tail = jnp.concatenate([tail, jnp.zeros((pad, TILE), F32)], 0)
    msg_ref[rows:] = tail.astype(I32)


def thirds(a):
    one = a.astype(BF16).astype(F32)
    two = (a - one).astype(BF16).astype(F32)
    return one, two, a - one - two


def point_features(points):
    a = (points - 0.5) * (1.0 / RADIUS)
    norm = a[0:1] * a[0:1] + a[1:2] * a[1:2] + a[2:3] * a[2:3]
    return thirds(a), jnp.concatenate(thirds(norm), 0)


def feature_kernel(vol_hbm, pts_hbm, coef_hbm, surf, vols, coefs, vol_ref, pts_ref, coef_ref, sems):
    copies = start_all(sems, (vol_hbm, vol_ref), (pts_hbm, pts_ref), (coef_hbm, coef_ref))
    n_local, group_tiles = surf.shape[0] - 1, vols.shape[0]
    step = 8
    ones = jnp.ones((3, step * TILE), F32)
    blank = jnp.zeros((FEATS - 24, step * TILE), F32)

    def surface(b, _):
        lanes = pl.ds(pl.multiple_of(b * step * TILE, step * TILE), step * TILE)
        (one, two, three), norm = point_features(pts_ref[:, lanes])
        one, two, three = -2.0 * one, -2.0 * two, -2.0 * three
        rows = jnp.concatenate([one, two, one, three, one, two, norm, ones, blank], 0).astype(BF16)
        coef = coef_ref[:, lanes] * 4.0
        high = coef.astype(BF16).astype(F32)
        pair = jnp.concatenate([high, coef - high, jnp.zeros((2, step * TILE), F32)], 0)
        for t in range(step):
            span = slice(t * TILE, (t + 1) * TILE)
            surf[b * step + t] = rows[:, span].T
            tile = pair[:, span].astype(BF16)
            coefs[b * step + t] = jnp.concatenate([tile, tile], 1)
        return 0

    surf[n_local] = jnp.zeros((TILE, FEATS), BF16)
    coefs[n_local] = jnp.zeros((8, 2 * TILE), BF16)

    def volume(b, _):
        lanes = pl.ds(pl.multiple_of(b * step * TILE, step * TILE), step * TILE)
        (one, two, three), norm = point_features(vol_ref[:, lanes])
        rows = jnp.concatenate([one, one, two, one, three, two, ones, norm, blank], 0).astype(BF16)
        for t in range(step):
            vols[b * step + t] = rows[:, t * TILE : (t + 1) * TILE]
        return 0

    copies[0].wait()
    lax.fori_loop(0, group_tiles // step, volume, 0)
    copies[1].wait()
    copies[2].wait()
    lax.fori_loop(0, n_local // step, surface, 0)


def main_kernel(n_col, n_local, list_rows, me_ref, *refs):
    msgs = refs[:n_col]
    surf, vols, coefs = refs[n_col : n_col + 3]
    outs = refs[n_col + 3 : 2 * n_col + 3]
    lists, past, now, acc, kern, sems = refs[2 * n_col + 3 :]
    msg_rows = msgs[0].shape[0]
    copies = start_all(
        sems, *((msgs[k], lists.at[pl.ds(k * msg_rows, msg_rows)]) for k in range(n_col))
    )
    acc[...] = jnp.zeros_like(acc)
    kern[...] = jnp.zeros_like(kern)
    group_tiles = vols.shape[0]
    bits = tile_bits(n_local)
    for c in copies:
        c.wait()
    me = me_ref[0]
    ends, shifts = [], []
    total = jnp.int32(0)
    for k in range(n_col):
        first = lists[k * msg_rows + list_rows + me, 0]
        last = lists[k * msg_rows + list_rows + me + 1, 0]
        shifts.append(k * msg_rows * TILE + first - total)
        total = total + (last - first)
        ends.append(total)

    def fetch(p):
        shift = shifts[0]
        for k in range(1, n_col):
            shift = jnp.where(p >= ends[k - 1], shifts[k], shift)
        valid = p < total
        at = jnp.where(valid, p + shift, 0)
        return jnp.where(valid, lists[at >> 7, at & (TILE - 1)], n_local)

    def parts(pair):
        return pair >> bits, pair & ((1 << bits) - 1)

    def move(pair, q):
        v, s = parts(pair)
        acc[v] += dot(coefs[s], kern[q])

    def evaluate(pair, q):
        v, s = parts(pair)
        squared = dot(surf[s], vols[v])
        squared = jnp.minimum(jnp.maximum(squared, 1e-12), 1.0)
        radius = squared * lax.rsqrt(squared)
        falloff = 1.0 - radius
        falloff = falloff * falloff
        value = falloff * falloff * (radius + 0.25)
        high = value.astype(BF16)
        kern[q, :TILE] = high
        kern[q, TILE:] = (value - high.astype(F32)).astype(BF16)

    for q in range(UNROLL):
        past[q] = n_local
        now[q] = fetch(jnp.int32(q))
    trips = (total + UNROLL - 1) // UNROLL

    def trip(h, _):
        for q in range(UNROLL):
            move(past[q], q)
            pair = now[q]
            evaluate(pair, q)
            past[q] = pair
            now[q] = fetch((h + 1) * UNROLL + q)
        return 0

    lax.fori_loop(0, trips, trip, 0)
    for q in range(UNROLL):
        move(past[q], q)

    share = group_tiles // n_col
    for k in range(n_col):
        base = lax.rem(me + k, n_col) * share
        for t in range(share):
            value = acc[base + t]
            outs[k][:, t * TILE : (t + 1) * TILE] = value[:3] + value[3:6]


def shift_right(x, k, n):
    return lax.ppermute(x, "col", [(i, (i + k) % n) for i in range(n)])


def per_device(vol_pts, surf_pts, surf_coef, vol_tile, slot, wanted, live):
    n_col = lax.axis_size("col")
    me = lax.axis_index("col").astype(I32).reshape(1)
    n_local = surf_pts.shape[1] // TILE
    group_tiles = vol_pts.shape[1] // TILE
    share = group_tiles // n_col
    list_rows = vol_tile.shape[1] // TILE
    msg_rows = -(-(list_rows + n_col + 2) // 8) * 8
    smem = pl.BlockSpec(memory_space=pltpu.SMEM)
    vmem = pl.BlockSpec(memory_space=pltpu.VMEM)
    hbm = pl.BlockSpec(memory_space=pltpu.HBM)

    def stay(x):
        return pltpu.with_memory_space_constraint(x, pltpu.HBM)

    msg = pl.pallas_call(
        functools.partial(sort_kernel, n_col, n_local),
        out_shape=jax.ShapeDtypeStruct((msg_rows, TILE), I32),
        in_specs=[smem, hbm, hbm, hbm],
        out_specs=vmem,
        scratch_shapes=[
            pltpu.VMEM((list_rows, TILE), I32),
            pltpu.VMEM((list_rows, TILE), I32),
            pltpu.VMEM(wanted.shape, I32),
            pltpu.SemaphoreType.DMA((3,)),
        ],
        compiler_params=pltpu.CompilerParams(vmem_limit_bytes=8 << 20),
        name="sort_pairs",
    )(live, stay(vol_tile.reshape(-1, TILE)), stay(slot.reshape(-1, TILE)), stay(wanted))
    msgs = [msg] + [shift_right(msg, k, n_col) for k in range(1, n_col)]
    features = pl.pallas_call(
        feature_kernel,
        out_shape=[
            jax.ShapeDtypeStruct((n_local + 1, TILE, FEATS), BF16),
            jax.ShapeDtypeStruct((group_tiles, FEATS, TILE), BF16),
            jax.ShapeDtypeStruct((n_local + 1, 8, 2 * TILE), BF16),
        ],
        in_specs=[hbm] * 3,
        out_specs=[vmem] * 3,
        scratch_shapes=[
            pltpu.VMEM(vol_pts.shape, F32),
            pltpu.VMEM(surf_pts.shape, F32),
            pltpu.VMEM(surf_coef.shape, F32),
            pltpu.SemaphoreType.DMA((3,)),
        ],
        compiler_params=pltpu.CompilerParams(vmem_limit_bytes=16 << 20),
        name="features",
    )(stay(vol_pts), stay(surf_pts), stay(surf_coef))
    parts = pl.pallas_call(
        functools.partial(main_kernel, n_col, n_local, list_rows),
        out_shape=[jax.ShapeDtypeStruct((3, share * TILE), F32)] * n_col,
        in_specs=[smem] + [vmem] * (n_col + 3),
        out_specs=[vmem] * n_col,
        scratch_shapes=[
            pltpu.SMEM((n_col * msg_rows, TILE), I32),
            pltpu.SMEM((UNROLL,), I32),
            pltpu.SMEM((UNROLL,), I32),
            pltpu.VMEM((group_tiles, 8, TILE), F32),
            pltpu.VMEM((UNROLL, 2 * TILE, TILE), BF16),
            pltpu.SemaphoreType.DMA((n_col,)),
        ],
        compiler_params=pltpu.CompilerParams(vmem_limit_bytes=32 << 20),
        name="pair_sums",
    )(me, *msgs, *features)
    out = parts[0]
    for k in range(1, n_col):
        out = out + shift_right(parts[k], k, n_col)
    return out


def solution(mesh):
    return jax.shard_map(
        per_device,
        mesh=mesh,
        in_specs=(
            P(None, ("gx", "gy")),
            P(None, "col"),
            P(None, "col"),
            P(("gx", "gy", "col"), None),
            P(("gx", "gy", "col"), None),
            P(("gx", "gy", "col"), None, None),
            P(("gx", "gy", "col")),
        ),
        out_specs=P(None, ("gx", "gy", "col")),
        check_vma=False,
    )
```

```python
import functools

import jax
import jax.numpy as jnp
from jax import lax
from jax.experimental import pallas as pl
from jax.experimental.pallas import tpu as pltpu
from jax.sharding import PartitionSpec as P

TILE = 128
RADIUS = 1.2
FEATS = 32
UNROLL = 32
CHUNK = 32
F32, BF16, I32 = jnp.float32, jnp.bfloat16, jnp.int32


def dot(a, b, contract=((1,), (0,))):
    return lax.dot_general(a, b, (contract, ((), ())), preferred_element_type=F32)


def tile_bits(n_local):
    return n_local.bit_length()


def iota(shape, axis):
    return lax.broadcasted_iota(I32, shape, axis)


def start_all(sems, *pairs):
    copies = [pltpu.make_async_copy(a, b, sems.at[k]) for k, (a, b) in enumerate(pairs)]
    for c in copies:
        c.start()
    return copies


def sort_kernel(
    n_col, n_local, share, live_ref, vol_hbm, slot_hbm, wanted_hbm, *refs
):
    inputs, (msg_ref, *copies_of) = refs[:3], refs[3:7]
    vol_ref, slot_ref, wanted_ref, sems, far_sems = refs[7:]
    near = start_all(sems, (vol_hbm, vol_ref), (slot_hbm, slot_ref), (wanted_hbm, wanted_ref))
    far = start_all(far_sems, *zip(inputs, copies_of))
    for c in near:
        c.wait()
    rows = vol_ref.shape[0]
    req = wanted_ref.shape[2]
    slot = slot_ref[...]
    vol = vol_ref[...].astype(F32)
    position = iota((rows, TILE), 0) * TILE + iota((rows, TILE), 1)
    peer, place = slot // req, slot % req
    key = 2 * peer + (vol_ref[...] // share == peer).astype(I32)
    key = jnp.where(position < live_ref[0], key, 2 * n_col)
    keys = 2 * n_col + 2
    masks = [(key == k).astype(F32) for k in range(keys)]
    mask = jnp.concatenate(masks, 0).astype(BF16)
    ahead = (iota((TILE, TILE), 0) < iota((TILE, TILE), 1)).astype(F32).astype(BF16)
    within = dot(mask, ahead)
    count = dot(mask, jnp.ones((TILE, TILE), BF16)).astype(BF16)
    total = keys * rows
    above = (iota((total, total), 1) < iota((total, total), 0)).astype(F32).astype(BF16)
    start = dot(above, count)
    rank = within + start
    dest = masks[0] * rank[:rows]
    for k in range(1, keys):
        dest += masks[k] * rank[k * rows : (k + 1) * rows]
    dest = dest.astype(I32)
    dest_row, dest_lane = dest // TILE, dest % TILE
    table = wanted_ref[0].astype(F32)
    if n_col % 8:
        table = jnp.concatenate([table, jnp.zeros((8 - n_col % 8, req), F32)], 0)
    table = table.astype(BF16)
    out = jnp.zeros((2 * rows, TILE), F32)
    for r in range(rows):
        row = slice(r, r + 1)
        chosen = (iota((req, TILE), 0) == place[row]).astype(F32).astype(BF16)
        tiles = dot(table, chosen)
        tiles = jnp.where(iota(tiles.shape, 0) == peer[row], tiles, 0.0)
        tile = jnp.sum(tiles, 0, keepdims=True)
        here = (iota((rows, TILE), 0) == dest_row[row]).astype(F32)
        values = jnp.concatenate([here * vol[row], here * tile], 0).astype(BF16)
        lanes = (iota((TILE, TILE), 0) == dest_lane[row]).astype(F32).astype(BF16)
        out += dot(values, lanes, ((1,), (1,)))
    out = out.astype(I32)
    msg_ref[:rows] = (out[:rows] << tile_bits(n_local)) | out[rows:]
    tail = jnp.concatenate([start[k * rows : k * rows + 1] for k in range(keys)], 0)
    pad = msg_ref.shape[0] - rows - keys
    if pad:
        tail = jnp.concatenate([tail, jnp.zeros((pad, TILE), F32)], 0)
    msg_ref[rows:] = tail.astype(I32)
    for c in far:
        c.wait()


def thirds(a):
    one = a.astype(BF16).astype(F32)
    two = (a - one).astype(BF16).astype(F32)
    return one, two, a - one - two


def point_features(points):
    a = (points - 0.5) * (1.0 / RADIUS)
    norm = a[0:1] * a[0:1] + a[1:2] * a[1:2] + a[2:3] * a[2:3]
    return thirds(a), jnp.concatenate(thirds(norm), 0)


def feature_kernel(vol_ref, pts_ref, coef_ref, surf, vols, coefs):
    n_local, group_tiles = surf.shape[0] - 1, vols.shape[0]
    step = min(32, n_local, group_tiles)
    ones = jnp.ones((3, step * TILE), F32)
    blank = jnp.zeros((FEATS - 24, step * TILE), F32)

    def surface(b, _):
        lanes = pl.ds(pl.multiple_of(b * step * TILE, step * TILE), step * TILE)
        (one, two, three), norm = point_features(pts_ref[:, lanes])
        one, two, three = -2.0 * one, -2.0 * two, -2.0 * three
        rows = jnp.concatenate([one, two, one, three, one, two, norm, ones, blank], 0).astype(BF16)
        coef = coef_ref[:, lanes] * 4.0
        high = coef.astype(BF16).astype(F32)
        pair = jnp.concatenate([high, coef - high, jnp.zeros((2, step * TILE), F32)], 0)
        for t in range(step):
            span = slice(t * TILE, (t + 1) * TILE)
            surf[b * step + t] = rows[:, span].T
            tile = pair[:, span].astype(BF16)
            coefs[b * step + t] = jnp.concatenate([tile, tile], 1)
        return 0

    surf[n_local] = jnp.zeros((TILE, FEATS), BF16)
    coefs[n_local] = jnp.zeros((8, 2 * TILE), BF16)

    def volume(b, _):
        lanes = pl.ds(pl.multiple_of(b * step * TILE, step * TILE), step * TILE)
        (one, two, three), norm = point_features(vol_ref[:, lanes])
        rows = jnp.concatenate([one, one, two, one, three, two, ones, norm, blank], 0).astype(BF16)
        for t in range(step):
            vols[b * step + t] = rows[:, t * TILE : (t + 1) * TILE]
        return 0

    lax.fori_loop(0, group_tiles // step, volume, 0)
    lax.fori_loop(0, n_local // step, surface, 0)


def main_kernel(n_col, n_local, list_rows, own, me_ref, *refs):
    msgs = refs[:n_col]
    surf, vols, coefs = refs[n_col : n_col + 3]
    targets = [0] if own else range(1, n_col)
    outs = refs[n_col + 3 :][: len(targets)]
    lists, past, now, acc, kern, sems = refs[n_col + 3 + len(targets) :]
    msg_rows = msgs[0].shape[0]
    copies = start_all(
        sems, *((msgs[k], lists.at[pl.ds(k * msg_rows, msg_rows)]) for k in range(n_col))
    )
    acc[...] = jnp.zeros_like(acc)
    kern[...] = jnp.zeros_like(kern)
    group_tiles = vols.shape[0]
    bits = tile_bits(n_local)
    for c in copies:
        c.wait()
    me = me_ref[0]
    ends, shifts = [], []
    total = jnp.int32(0)
    for k in range(n_col):
        first = lists[k * msg_rows + list_rows + 2 * me + own, 0]
        last = lists[k * msg_rows + list_rows + 2 * me + own + 1, 0]
        shifts.append(k * msg_rows * TILE + first - total)
        total = total + (last - first)
        ends.append(total)

    def fetch(p):
        shift = shifts[0]
        for k in range(1, n_col):
            shift = jnp.where(p >= ends[k - 1], shifts[k], shift)
        valid = p < total
        at = jnp.where(valid, p + shift, 0)
        return jnp.where(valid, lists[at >> 7, at & (TILE - 1)], n_local)

    def parts(pair):
        return pair >> bits, pair & ((1 << bits) - 1)

    def move(pair, q):
        v, s = parts(pair)
        acc[v] += dot(coefs[s], kern[q])

    def evaluate(pair, q):
        v, s = parts(pair)
        for c in range(0, TILE, CHUNK):
            squared = dot(surf[s, c : c + CHUNK], vols[v])
            squared = jnp.minimum(jnp.maximum(squared, 1e-12), 1.0)
            radius = squared * lax.rsqrt(squared)
            falloff = 1.0 - radius
            falloff = falloff * falloff
            value = falloff * falloff * (radius + 0.25)
            high = value.astype(BF16)
            kern[q, c : c + CHUNK] = high
            kern[q, TILE + c : TILE + c + CHUNK] = (value - high.astype(F32)).astype(BF16)

    for q in range(UNROLL):
        past[q] = n_local
        now[q] = fetch(jnp.int32(q))
    trips = (total + UNROLL - 1) // UNROLL

    def trip(h, _):
        for q in range(UNROLL):
            move(past[q], q)
            pair = now[q]
            evaluate(pair, q)
            past[q] = pair
            now[q] = fetch((h + 1) * UNROLL + q)
        return 0

    lax.fori_loop(0, trips, trip, 0)
    for q in range(UNROLL):
        move(past[q], q)

    share = group_tiles // n_col
    for out, k in zip(outs, targets):
        base = lax.rem(me + k, n_col) * share
        for t in range(share):
            value = acc[base + t]
            out[:, t * TILE : (t + 1) * TILE] = value[:3] + value[3:6]


def shift_right(x, k, n):
    return lax.ppermute(x, "col", [(i, (i + k) % n) for i in range(n)])


def per_device(vol_pts, surf_pts, surf_coef, vol_tile, slot, wanted, live):
    n_col = lax.axis_size("col")
    me = lax.axis_index("col").astype(I32).reshape(1)
    n_local = surf_pts.shape[1] // TILE
    group_tiles = vol_pts.shape[1] // TILE
    share = group_tiles // n_col
    list_rows = vol_tile.shape[1] // TILE
    msg_rows = -(-(list_rows + 2 * n_col + 2) // 8) * 8
    smem = pl.BlockSpec(memory_space=pltpu.SMEM)
    vmem = pl.BlockSpec(memory_space=pltpu.VMEM)
    hbm = pl.BlockSpec(memory_space=pltpu.HBM)

    def stay(x):
        return pltpu.with_memory_space_constraint(x, pltpu.HBM)

    inputs = (vol_pts, surf_pts, surf_coef)
    msg, *near = pl.pallas_call(
        functools.partial(sort_kernel, n_col, n_local, share),
        out_shape=[jax.ShapeDtypeStruct((msg_rows, TILE), I32)]
        + [jax.ShapeDtypeStruct(x.shape, x.dtype) for x in inputs],
        in_specs=[smem] + [hbm] * 6,
        out_specs=[vmem] * 4,
        scratch_shapes=[
            pltpu.VMEM((list_rows, TILE), I32),
            pltpu.VMEM((list_rows, TILE), I32),
            pltpu.VMEM(wanted.shape, I32),
            pltpu.SemaphoreType.DMA((3,)),
            pltpu.SemaphoreType.DMA((3,)),
        ],
        compiler_params=pltpu.CompilerParams(vmem_limit_bytes=8 << 20),
        name="sort_pairs",
    )(live, *map(stay, (vol_tile.reshape(-1, TILE), slot.reshape(-1, TILE), wanted, *inputs)))
    msgs = [msg] + [shift_right(msg, k, n_col) for k in range(1, n_col)]
    features = pl.pallas_call(
        feature_kernel,
        out_shape=[
            jax.ShapeDtypeStruct((n_local + 1, TILE, FEATS), BF16),
            jax.ShapeDtypeStruct((group_tiles, FEATS, TILE), BF16),
            jax.ShapeDtypeStruct((n_local + 1, 8, 2 * TILE), BF16),
        ],
        in_specs=[vmem] * 3,
        out_specs=[vmem] * 3,
        compiler_params=pltpu.CompilerParams(vmem_limit_bytes=16 << 20),
        name="features",
    )(*near)
    def sums(own, count):
        return pl.pallas_call(
            functools.partial(main_kernel, n_col, n_local, list_rows, own),
            out_shape=[jax.ShapeDtypeStruct((3, share * TILE), F32)] * count,
            in_specs=[smem] + [vmem] * (n_col + 3),
            out_specs=[vmem] * count,
            scratch_shapes=[
                pltpu.SMEM((n_col * msg_rows, TILE), I32),
                pltpu.SMEM((UNROLL,), I32),
                pltpu.SMEM((UNROLL,), I32),
                pltpu.VMEM((group_tiles, 8, TILE), F32),
                pltpu.VMEM((UNROLL, 2 * TILE, TILE), BF16),
                pltpu.SemaphoreType.DMA((n_col,)),
            ],
            compiler_params=pltpu.CompilerParams(vmem_limit_bytes=16 << 20),
            name="pair_sums_own" if own else "pair_sums_sent",
        )(me, *msgs, *features)

    sent = [shift_right(x, k, n_col) for k, x in enumerate(sums(0, n_col - 1), 1)]
    (out,) = sums(1, 1)
    for x in sent:
        out = out + x
    return out


def solution(mesh):
    return jax.shard_map(
        per_device,
        mesh=mesh,
        in_specs=(
            P(None, ("gx", "gy")),
            P(None, "col"),
            P(None, "col"),
            P(("gx", "gy", "col"), None),
            P(("gx", "gy", "col"), None),
            P(("gx", "gy", "col"), None, None),
            P(("gx", "gy", "col")),
        ),
        out_specs=P(None, ("gx", "gy", "col")),
        check_vma=False,
    )
```

```python
import functools

import jax
import jax.numpy as jnp
from jax import lax
from jax.experimental import pallas as pl
from jax.experimental.pallas import tpu as pltpu
from jax.sharding import PartitionSpec as P

TILE = 128
RADIUS = 1.2
FEATS = 32
UNROLL = 32
AHEAD = 3
BEHIND = 6
F32, BF16, I32 = jnp.float32, jnp.bfloat16, jnp.int32


def dot(a, b, contract=((1,), (0,))):
    return lax.dot_general(a, b, (contract, ((), ())), preferred_element_type=F32)


def tile_bits(n_local):
    return n_local.bit_length()


def iota(shape, axis):
    return lax.broadcasted_iota(I32, shape, axis)


def start_all(sems, *pairs):
    copies = [pltpu.make_async_copy(a, b, sems.at[k]) for k, (a, b) in enumerate(pairs)]
    for c in copies:
        c.start()
    return copies


def sort_kernel(
    n_col, n_local, share, live_ref, vol_hbm, slot_hbm, wanted_hbm, *refs
):
    inputs, (msg_ref, *copies_of) = refs[:3], refs[3:7]
    vol_ref, slot_ref, wanted_ref, sems, far_sems = refs[7:]
    near = start_all(sems, (vol_hbm, vol_ref), (slot_hbm, slot_ref), (wanted_hbm, wanted_ref))
    far = start_all(far_sems, *zip(inputs, copies_of))
    for c in near:
        c.wait()
    rows = vol_ref.shape[0]
    req = wanted_ref.shape[2]
    slot = slot_ref[...]
    vol = vol_ref[...].astype(F32)
    position = iota((rows, TILE), 0) * TILE + iota((rows, TILE), 1)
    peer, place = slot // req, slot % req
    key = 2 * peer + (vol_ref[...] // share == peer).astype(I32)
    key = jnp.where(position < live_ref[0], key, 2 * n_col)
    keys = 2 * n_col + 2
    masks = [(key == k).astype(F32) for k in range(keys)]
    mask = jnp.concatenate(masks, 0).astype(BF16)
    ahead = (iota((TILE, TILE), 0) < iota((TILE, TILE), 1)).astype(F32).astype(BF16)
    within = dot(mask, ahead)
    count = dot(mask, jnp.ones((TILE, TILE), BF16)).astype(BF16)
    total = keys * rows
    above = (iota((total, total), 1) < iota((total, total), 0)).astype(F32).astype(BF16)
    start = dot(above, count)
    rank = within + start
    dest = masks[0] * rank[:rows]
    for k in range(1, keys):
        dest += masks[k] * rank[k * rows : (k + 1) * rows]
    dest = dest.astype(I32)
    dest_row, dest_lane = dest // TILE, dest % TILE
    table = wanted_ref[0].astype(F32)
    if n_col % 8:
        table = jnp.concatenate([table, jnp.zeros((8 - n_col % 8, req), F32)], 0)
    table = table.astype(BF16)
    out = jnp.zeros((2 * rows, TILE), F32)
    for r in range(rows):
        row = slice(r, r + 1)
        chosen = (iota((req, TILE), 0) == place[row]).astype(F32).astype(BF16)
        tiles = dot(table, chosen)
        tiles = jnp.where(iota(tiles.shape, 0) == peer[row], tiles, 0.0)
        tile = jnp.sum(tiles, 0, keepdims=True)
        here = (iota((rows, TILE), 0) == dest_row[row]).astype(F32)
        values = jnp.concatenate([here * vol[row], here * tile], 0).astype(BF16)
        lanes = (iota((TILE, TILE), 0) == dest_lane[row]).astype(F32).astype(BF16)
        out += dot(values, lanes, ((1,), (1,)))
    out = out.astype(I32)
    msg_ref[:rows] = (out[:rows] << tile_bits(n_local)) | out[rows:]
    even, odd = (
        jnp.concatenate([start[k * rows : k * rows + 1] for k in range(first, keys, 2)], 0)
        for first in (0, 1)
    )
    tail = jnp.where(iota(even.shape, 1) < TILE // 2, even, odd)
    pad = msg_ref.shape[0] - rows - keys // 2
    if pad:
        tail = jnp.concatenate([tail, jnp.zeros((pad, TILE), F32)], 0)
    msg_ref[rows:] = tail.astype(I32)
    for c in far:
        c.wait()


def thirds(a):
    one = a.astype(BF16).astype(F32)
    two = (a - one).astype(BF16).astype(F32)
    return one, two, a - one - two


def point_features(points):
    a = (points - 0.5) * (1.0 / RADIUS)
    norm = a[0:1] * a[0:1] + a[1:2] * a[1:2] + a[2:3] * a[2:3]
    return thirds(a), jnp.concatenate(thirds(norm), 0)


def feature_kernel(vol_ref, pts_ref, coef_ref, surf, vols, coefs):
    n_local, group_tiles = surf.shape[0] - 1, vols.shape[0]
    step = min(32, n_local, group_tiles)
    ones = jnp.ones((3, step * TILE), F32)
    blank = jnp.zeros((FEATS - 24, step * TILE), F32)

    def surface(b, _):
        lanes = pl.ds(pl.multiple_of(b * step * TILE, step * TILE), step * TILE)
        (one, two, three), norm = point_features(pts_ref[:, lanes])
        one, two, three = -2.0 * one, -2.0 * two, -2.0 * three
        rows = jnp.concatenate([one, two, one, three, one, two, norm, ones, blank], 0).astype(BF16)
        coef = coef_ref[:, lanes] * 4.0
        high = coef.astype(BF16).astype(F32)
        pair = jnp.concatenate([high, coef - high, jnp.zeros((2, step * TILE), F32)], 0)
        for t in range(step):
            span = slice(t * TILE, (t + 1) * TILE)
            surf[b * step + t] = rows[:, span].T
            tile = pair[:, span].astype(BF16)
            coefs[b * step + t] = jnp.concatenate([tile, tile], 1)
        return 0

    surf[n_local] = jnp.zeros((TILE, FEATS), BF16)
    coefs[n_local] = jnp.zeros((8, 2 * TILE), BF16)

    def volume(b, _):
        lanes = pl.ds(pl.multiple_of(b * step * TILE, step * TILE), step * TILE)
        (one, two, three), norm = point_features(vol_ref[:, lanes])
        rows = jnp.concatenate([one, one, two, one, three, two, ones, norm, blank], 0).astype(BF16)
        for t in range(step):
            vols[b * step + t] = rows[:, t * TILE : (t + 1) * TILE]
        return 0

    lax.fori_loop(0, group_tiles // step, volume, 0)
    lax.fori_loop(0, n_local // step, surface, 0)


def main_kernel(n_col, n_local, list_rows, own, me_ref, *refs):
    msgs = refs[:n_col]
    surf, vols, coefs = refs[n_col : n_col + 3]
    targets = [0] if own else range(1, n_col)
    outs = refs[n_col + 3 :][: len(targets)]
    lists, past, now, acc, dist, kern, sems = refs[n_col + 3 + len(targets) :]
    msg_rows = msgs[0].shape[0]
    copies = start_all(
        sems, *((msgs[k], lists.at[pl.ds(k * msg_rows, msg_rows)]) for k in range(n_col))
    )
    acc[...] = jnp.zeros_like(acc)
    kern[UNROLL - BEHIND :] = jnp.zeros((BEHIND, 2 * TILE, TILE), BF16)
    group_tiles = vols.shape[0]
    bits = tile_bits(n_local)
    for c in copies:
        c.wait()
    me = me_ref[0]
    ends, shifts = [], []
    total = jnp.int32(0)
    for k in range(n_col):
        row = k * msg_rows + list_rows + me
        first = lists[row, own * TILE // 2]
        last = lists[row + own, (1 - own) * TILE // 2]
        shifts.append(k * msg_rows * TILE + first - total)
        total = total + (last - first)
        ends.append(total)

    def fetch(p):
        shift = shifts[0]
        for k in range(1, n_col):
            shift = jnp.where(p >= ends[k - 1], shifts[k], shift)
        valid = p < total
        at = jnp.where(valid, p + shift, 0)
        return jnp.where(valid, lists[at >> 7, at & (TILE - 1)], n_local)

    def parts(pair):
        return pair >> bits, pair & ((1 << bits) - 1)

    def move(pair, q):
        v, s = parts(pair)
        acc[v] += dot(coefs[s], kern[q])

    def distance(pair):
        v, s = parts(pair)
        return dot(surf[s], vols[v])

    def evaluate(squared, q):
        squared = jnp.minimum(jnp.maximum(squared, 1e-12), 1.0)
        radius = squared * lax.rsqrt(squared)
        falloff = 1.0 - radius
        falloff = falloff * falloff
        value = falloff * falloff * (radius + 0.25)
        high = value.astype(BF16)
        kern[q, :TILE] = high
        kern[q, TILE:] = (value - high.astype(F32)).astype(BF16)

    for q in range(UNROLL):
        now[q] = fetch(jnp.int32(q))
    for q in range(BEHIND):
        past[q] = n_local
    for q in range(AHEAD):
        dist[q] = distance(now[q])
    trips = (total + UNROLL - 1) // UNROLL

    def trip(h, _):
        pairs = []
        squared = [dist[q] for q in range(AHEAD)]
        for q in range(UNROLL):
            pairs.append(now[q])
            now[q] = fetch((h + 1) * UNROLL + q)
            ahead = distance(now[(q + AHEAD) % UNROLL])
            if q + AHEAD < UNROLL:
                squared.append(ahead)
            else:
                dist[q + AHEAD - UNROLL] = ahead
            move(pairs[q - BEHIND] if q >= BEHIND else past[q], (q - BEHIND) % UNROLL)
            evaluate(squared[q], q)
        for q in range(BEHIND):
            past[q] = pairs[UNROLL - BEHIND + q]
        return 0

    lax.fori_loop(0, trips, trip, 0)
    for q in range(BEHIND):
        move(past[q], UNROLL - BEHIND + q)

    share = group_tiles // n_col
    for out, k in zip(outs, targets):
        base = lax.rem(me + k, n_col) * share
        for t in range(share):
            value = acc[base + t]
            out[:, t * TILE : (t + 1) * TILE] = value[:3] + value[3:6]


def shift_right(x, k, n):
    return lax.ppermute(x, "col", [(i, (i + k) % n) for i in range(n)])


def per_device(vol_pts, surf_pts, surf_coef, vol_tile, slot, wanted, live):
    n_col = lax.axis_size("col")
    me = lax.axis_index("col").astype(I32).reshape(1)
    n_local = surf_pts.shape[1] // TILE
    group_tiles = vol_pts.shape[1] // TILE
    share = group_tiles // n_col
    list_rows = vol_tile.shape[1] // TILE
    msg_rows = -(-(list_rows + n_col + 1) // 8) * 8
    smem = pl.BlockSpec(memory_space=pltpu.SMEM)
    vmem = pl.BlockSpec(memory_space=pltpu.VMEM)
    hbm = pl.BlockSpec(memory_space=pltpu.HBM)

    def stay(x):
        return pltpu.with_memory_space_constraint(x, pltpu.HBM)

    inputs = (vol_pts, surf_pts, surf_coef)
    msg, *near = pl.pallas_call(
        functools.partial(sort_kernel, n_col, n_local, share),
        out_shape=[jax.ShapeDtypeStruct((msg_rows, TILE), I32)]
        + [jax.ShapeDtypeStruct(x.shape, x.dtype) for x in inputs],
        in_specs=[smem] + [hbm] * 6,
        out_specs=[vmem] * 4,
        scratch_shapes=[
            pltpu.VMEM((list_rows, TILE), I32),
            pltpu.VMEM((list_rows, TILE), I32),
            pltpu.VMEM(wanted.shape, I32),
            pltpu.SemaphoreType.DMA((3,)),
            pltpu.SemaphoreType.DMA((3,)),
        ],
        compiler_params=pltpu.CompilerParams(vmem_limit_bytes=8 << 20),
        name="sort_pairs",
    )(live, *map(stay, (vol_tile.reshape(-1, TILE), slot.reshape(-1, TILE), wanted, *inputs)))
    msgs = [msg] + [shift_right(msg, k, n_col) for k in range(1, n_col)]
    features = pl.pallas_call(
        feature_kernel,
        out_shape=[
            jax.ShapeDtypeStruct((n_local + 1, TILE, FEATS), BF16),
            jax.ShapeDtypeStruct((group_tiles, FEATS, TILE), BF16),
            jax.ShapeDtypeStruct((n_local + 1, 8, 2 * TILE), BF16),
        ],
        in_specs=[vmem] * 3,
        out_specs=[vmem] * 3,
        compiler_params=pltpu.CompilerParams(vmem_limit_bytes=16 << 20),
        name="features",
    )(*near)
    def sums(own, count):
        return pl.pallas_call(
            functools.partial(main_kernel, n_col, n_local, list_rows, own),
            out_shape=[jax.ShapeDtypeStruct((3, share * TILE), F32)] * count,
            in_specs=[smem] + [vmem] * (n_col + 3),
            out_specs=[vmem] * count,
            scratch_shapes=[
                pltpu.SMEM((n_col * msg_rows, TILE), I32),
                pltpu.SMEM((BEHIND,), I32),
                pltpu.SMEM((UNROLL,), I32),
                pltpu.VMEM((group_tiles, 8, TILE), F32),
                pltpu.VMEM((AHEAD, TILE, TILE), F32),
                pltpu.VMEM((UNROLL, 2 * TILE, TILE), BF16),
                pltpu.SemaphoreType.DMA((n_col,)),
            ],
            compiler_params=pltpu.CompilerParams(vmem_limit_bytes=16 << 20),
            name="pair_sums_own" if own else "pair_sums_sent",
        )(me, *msgs, *features)

    sent = [shift_right(x, k, n_col) for k, x in enumerate(sums(0, n_col - 1), 1)]
    (out,) = sums(1, 1)
    for x in sent:
        out = out + x
    return out


def solution(mesh):
    return jax.shard_map(
        per_device,
        mesh=mesh,
        in_specs=(
            P(None, ("gx", "gy")),
            P(None, "col"),
            P(None, "col"),
            P(("gx", "gy", "col"), None),
            P(("gx", "gy", "col"), None),
            P(("gx", "gy", "col"), None, None),
            P(("gx", "gy", "col")),
        ),
        out_specs=P(None, ("gx", "gy", "col")),
        check_vma=False,
    )
```

```python
import functools

import jax
import jax.numpy as jnp
from jax import lax
from jax.experimental import pallas as pl
from jax.experimental.pallas import tpu as pltpu
from jax.sharding import PartitionSpec as P

TILE = 128
RADIUS = 1.2
FEATS = 32
UNROLL = 32
AHEAD = 3
BEHIND = 6
F32, BF16, I32 = jnp.float32, jnp.bfloat16, jnp.int32


def dot(a, b, contract=((1,), (0,))):
    return lax.dot_general(a, b, (contract, ((), ())), preferred_element_type=F32)


def tile_bits(n_local):
    return n_local.bit_length()


def iota(shape, axis):
    return lax.broadcasted_iota(I32, shape, axis)


def start_all(sems, *pairs):
    copies = [pltpu.make_async_copy(a, b, sems.at[k]) for k, (a, b) in enumerate(pairs)]
    for c in copies:
        c.start()
    return copies


def sort_kernel(
    n_col, share, live_ref, vol_hbm, slot_hbm, wanted_hbm, *refs
):
    inputs, (msg_ref, *copies_of) = refs[:3], refs[3:7]
    vol_ref, slot_ref, wanted_ref, sems, far_sems = refs[7:]
    near = start_all(sems, (vol_hbm, vol_ref), (slot_hbm, slot_ref), (wanted_hbm, wanted_ref))
    far = start_all(far_sems, *zip(inputs, copies_of))
    for c in near:
        c.wait()
    rows = vol_ref.shape[0]
    req = wanted_ref.shape[2]
    slot = slot_ref[...]
    vol = vol_ref[...].astype(F32)
    position = iota((rows, TILE), 0) * TILE + iota((rows, TILE), 1)
    peer, place = slot // req, slot % req
    key = 2 * peer + (vol_ref[...] // share == peer).astype(I32)
    key = jnp.where(position < live_ref[0], key, 2 * n_col)
    keys = 2 * n_col + 2
    masks = [(key == k).astype(F32) for k in range(keys)]
    mask = jnp.concatenate(masks, 0).astype(BF16)
    ahead = (iota((TILE, TILE), 0) < iota((TILE, TILE), 1)).astype(F32).astype(BF16)
    within = dot(mask, ahead)
    count = dot(mask, jnp.ones((TILE, TILE), BF16)).astype(BF16)
    total = keys * rows
    above = (iota((total, total), 1) < iota((total, total), 0)).astype(F32).astype(BF16)
    start = dot(above, count)
    rank = within + start
    dest = masks[0] * rank[:rows]
    for k in range(1, keys):
        dest += masks[k] * rank[k * rows : (k + 1) * rows]
    dest = dest.astype(I32)
    dest_row, dest_lane = dest // TILE, dest % TILE
    table = wanted_ref[0].astype(F32)
    if n_col % 8:
        table = jnp.concatenate([table, jnp.zeros((8 - n_col % 8, req), F32)], 0)
    table = table.astype(BF16)
    out = jnp.zeros((2 * rows, TILE), F32)
    for r in range(rows):
        row = slice(r, r + 1)
        chosen = (iota((req, TILE), 0) == place[row]).astype(F32).astype(BF16)
        tiles = dot(table, chosen)
        tiles = jnp.where(iota(tiles.shape, 0) == peer[row], tiles, 0.0)
        tile = jnp.sum(tiles, 0, keepdims=True)
        here = (iota((rows, TILE), 0) == dest_row[row]).astype(F32)
        values = jnp.concatenate([here * vol[row], here * tile], 0).astype(BF16)
        lanes = (iota((TILE, TILE), 0) == dest_lane[row]).astype(F32).astype(BF16)
        out += dot(values, lanes, ((1,), (1,)))
    msg_ref[: 2 * rows] = out.astype(I32)
    even, odd = (
        jnp.concatenate([start[k * rows : k * rows + 1] for k in range(first, keys, 2)], 0)
        for first in (0, 1)
    )
    tail = jnp.where(iota(even.shape, 1) < TILE // 2, even, odd)
    pad = msg_ref.shape[0] - 2 * rows - keys // 2
    if pad:
        tail = jnp.concatenate([tail, jnp.zeros((pad, TILE), F32)], 0)
    msg_ref[2 * rows :] = tail.astype(I32)
    for c in far:
        c.wait()


def thirds(a):
    one = a.astype(BF16).astype(F32)
    two = (a - one).astype(BF16).astype(F32)
    return one, two, a - one - two


def point_features(points):
    a = (points - 0.5) * (1.0 / RADIUS)
    norm = a[0:1] * a[0:1] + a[1:2] * a[1:2] + a[2:3] * a[2:3]
    return thirds(a), jnp.concatenate(thirds(norm), 0)


def feature_kernel(vol_ref, pts_ref, coef_ref, surf, vols, coefs):
    n_local, group_tiles = surf.shape[0] - 1, vols.shape[0]
    step = min(32, n_local, group_tiles)
    ones = jnp.ones((3, step * TILE), F32)
    blank = jnp.zeros((FEATS - 24, step * TILE), F32)

    def surface(b, _):
        lanes = pl.ds(pl.multiple_of(b * step * TILE, step * TILE), step * TILE)
        (one, two, three), norm = point_features(pts_ref[:, lanes])
        one, two, three = -2.0 * one, -2.0 * two, -2.0 * three
        rows = jnp.concatenate([one, two, one, three, one, two, norm, ones, blank], 0).astype(BF16)
        coef = coef_ref[:, lanes] * 4.0
        high = coef.astype(BF16).astype(F32)
        pair = jnp.concatenate([high, coef - high, jnp.zeros((2, step * TILE), F32)], 0)
        for t in range(step):
            span = slice(t * TILE, (t + 1) * TILE)
            surf[b * step + t] = rows[:, span].T
            tile = pair[:, span].astype(BF16)
            coefs[b * step + t] = jnp.concatenate([tile, tile], 1)
        return 0

    surf[n_local] = jnp.zeros((TILE, FEATS), BF16)
    coefs[n_local] = jnp.zeros((8, 2 * TILE), BF16)

    def volume(b, _):
        lanes = pl.ds(pl.multiple_of(b * step * TILE, step * TILE), step * TILE)
        (one, two, three), norm = point_features(vol_ref[:, lanes])
        rows = jnp.concatenate([one, one, two, one, three, two, ones, norm, blank], 0).astype(BF16)
        for t in range(step):
            vols[b * step + t] = rows[:, t * TILE : (t + 1) * TILE]
        return 0

    lax.fori_loop(0, group_tiles // step, volume, 0)
    lax.fori_loop(0, n_local // step, surface, 0)


def main_kernel(n_col, n_local, rows, own, me_ref, *refs):
    msgs = refs[:n_col]
    surf, vols, coefs = refs[n_col : n_col + 3]
    targets = [0] if own else range(n_col)
    outs = refs[n_col + 3 :][: len(targets)]
    packed, lists, past, now, acc, dist, kern, sem = refs[n_col + 3 + len(targets) :]
    group_tiles = vols.shape[0]
    bits = tile_bits(n_local)
    me = me_ref[0]
    for k, msg in enumerate(msgs):
        packed[k * rows : (k + 1) * rows] = (msg[:rows] << bits) | msg[rows : 2 * rows]
        at = n_col * rows + 2 * k
        packed[at : at + 2] = msg[pl.ds(2 * rows + me, 2)]
    copy = pltpu.make_async_copy(packed, lists, sem)
    copy.start()
    acc[...] = jnp.zeros_like(acc)
    kern[UNROLL - BEHIND :] = jnp.zeros((BEHIND, 2 * TILE, TILE), BF16)
    copy.wait()
    bounds = []
    for k in range(n_col):
        at = n_col * rows + 2 * k
        bounds.append((lists[at, 0], lists[at, TILE // 2], lists[at + 1, 0]))
    ends, shifts = [], []
    total = jnp.int32(0)
    for part in range(2):
        for k in range(n_col):
            first, last = bounds[k][part], bounds[k][part + 1]
            shifts.append(k * rows * TILE + first - total)
            total = total + (last - first)
            ends.append(total)
    whole = (ends[n_col - 1] + UNROLL - 1) // UNROLL
    begin, end = (whole, (total + UNROLL - 1) // UNROLL) if own else (0, whole)

    def fetch(p):
        shift = shifts[0]
        for k in range(1, 2 * n_col):
            shift = jnp.where(p >= ends[k - 1], shifts[k], shift)
        valid = p < total
        at = jnp.where(valid, p + shift, 0)
        return jnp.where(valid, lists[at >> 7, at & (TILE - 1)], n_local)

    def parts(pair):
        return pair >> bits, pair & ((1 << bits) - 1)

    def move(pair, q):
        v, s = parts(pair)
        acc[v] += dot(coefs[s], kern[q])

    def distance(pair):
        v, s = parts(pair)
        return dot(surf[s], vols[v])

    def evaluate(squared, q):
        squared = jnp.minimum(jnp.maximum(squared, 1e-12), 1.0)
        radius = squared * lax.rsqrt(squared)
        falloff = 1.0 - radius
        falloff = falloff * falloff
        value = falloff * falloff * (radius + 0.25)
        high = value.astype(BF16)
        kern[q, :TILE] = high
        kern[q, TILE:] = (value - high.astype(F32)).astype(BF16)

    for q in range(UNROLL):
        now[q] = fetch(begin * UNROLL + q)
    for q in range(BEHIND):
        past[q] = n_local
    for q in range(AHEAD):
        dist[q] = distance(now[q])

    def trip(h, _):
        pairs = []
        squared = [dist[q] for q in range(AHEAD)]
        for q in range(UNROLL):
            pairs.append(now[q])
            now[q] = fetch((h + 1) * UNROLL + q)
            ahead = distance(now[(q + AHEAD) % UNROLL])
            if q + AHEAD < UNROLL:
                squared.append(ahead)
            else:
                dist[q + AHEAD - UNROLL] = ahead
            move(pairs[q - BEHIND] if q >= BEHIND else past[q], (q - BEHIND) % UNROLL)
            evaluate(squared[q], q)
        for q in range(BEHIND):
            past[q] = pairs[UNROLL - BEHIND + q]
        return 0

    lax.fori_loop(begin, end, trip, 0)
    for q in range(BEHIND):
        move(past[q], UNROLL - BEHIND + q)

    share = group_tiles // n_col
    for out, k in zip(outs, targets):
        base = lax.rem(me + k, n_col) * share
        for t in range(share):
            value = acc[base + t]
            out[:, t * TILE : (t + 1) * TILE] = value[:3] + value[3:6]


def shift_right(x, k, n):
    return lax.ppermute(x, "col", [(i, (i + k) % n) for i in range(n)])


def per_device(vol_pts, surf_pts, surf_coef, vol_tile, slot, wanted, live):
    n_col = lax.axis_size("col")
    me = lax.axis_index("col").astype(I32).reshape(1)
    n_local = surf_pts.shape[1] // TILE
    group_tiles = vol_pts.shape[1] // TILE
    share = group_tiles // n_col
    list_rows = vol_tile.shape[1] // TILE
    msg_rows = -(-(2 * list_rows + n_col + 1) // 8) * 8
    packed_rows = -(-(n_col * list_rows + 2 * n_col) // 8) * 8
    smem = pl.BlockSpec(memory_space=pltpu.SMEM)
    vmem = pl.BlockSpec(memory_space=pltpu.VMEM)
    hbm = pl.BlockSpec(memory_space=pltpu.HBM)

    def stay(x):
        return pltpu.with_memory_space_constraint(x, pltpu.HBM)

    inputs = (vol_pts, surf_pts, surf_coef)
    msg, *near = pl.pallas_call(
        functools.partial(sort_kernel, n_col, share),
        out_shape=[jax.ShapeDtypeStruct((msg_rows, TILE), I32)]
        + [jax.ShapeDtypeStruct(x.shape, x.dtype) for x in inputs],
        in_specs=[smem] + [hbm] * 6,
        out_specs=[vmem] * 4,
        scratch_shapes=[
            pltpu.VMEM((list_rows, TILE), I32),
            pltpu.VMEM((list_rows, TILE), I32),
            pltpu.VMEM(wanted.shape, I32),
            pltpu.SemaphoreType.DMA((3,)),
            pltpu.SemaphoreType.DMA((3,)),
        ],
        compiler_params=pltpu.CompilerParams(vmem_limit_bytes=8 << 20),
        name="sort_pairs",
    )(live, *map(stay, (vol_tile.reshape(-1, TILE), slot.reshape(-1, TILE), wanted, *inputs)))
    msgs = [msg] + [shift_right(msg, k, n_col) for k in range(1, n_col)]
    features = pl.pallas_call(
        feature_kernel,
        out_shape=[
            jax.ShapeDtypeStruct((n_local + 1, TILE, FEATS), BF16),
            jax.ShapeDtypeStruct((group_tiles, FEATS, TILE), BF16),
            jax.ShapeDtypeStruct((n_local + 1, 8, 2 * TILE), BF16),
        ],
        in_specs=[vmem] * 3,
        out_specs=[vmem] * 3,
        compiler_params=pltpu.CompilerParams(vmem_limit_bytes=16 << 20),
        name="features",
    )(*near)
    def sums(own, count):
        return pl.pallas_call(
            functools.partial(main_kernel, n_col, n_local, list_rows, own),
            out_shape=[jax.ShapeDtypeStruct((3, share * TILE), F32)] * count,
            in_specs=[smem] + [vmem] * (n_col + 3),
            out_specs=[vmem] * count,
            scratch_shapes=[
                pltpu.VMEM((packed_rows, TILE), I32),
                pltpu.SMEM((packed_rows, TILE), I32),
                pltpu.SMEM((BEHIND,), I32),
                pltpu.SMEM((UNROLL,), I32),
                pltpu.VMEM((group_tiles, 8, TILE), F32),
                pltpu.VMEM((AHEAD, TILE, TILE), F32),
                pltpu.VMEM((UNROLL, 2 * TILE, TILE), BF16),
                pltpu.SemaphoreType.DMA,
            ],
            compiler_params=pltpu.CompilerParams(vmem_limit_bytes=16 << 20),
            name="pair_sums_own" if own else "pair_sums_sent",
        )(me, *msgs, *features)

    out, *sent = sums(0, n_col)
    sent = [shift_right(x, k, n_col) for k, x in enumerate(sent, 1)]
    for x in (*sums(1, 1), *sent):
        out = out + x
    return out


def solution(mesh):
    return jax.shard_map(
        per_device,
        mesh=mesh,
        in_specs=(
            P(None, ("gx", "gy")),
            P(None, "col"),
            P(None, "col"),
            P(("gx", "gy", "col"), None),
            P(("gx", "gy", "col"), None),
            P(("gx", "gy", "col"), None, None),
            P(("gx", "gy", "col")),
        ),
        out_specs=P(None, ("gx", "gy", "col")),
        check_vma=False,
    )
```

```python
import functools

import jax
import jax.numpy as jnp
from jax import lax
from jax.experimental import pallas as pl
from jax.experimental.pallas import tpu as pltpu
from jax.sharding import PartitionSpec as P

TILE = 128
RADIUS = 1.2
FEATS = 32
UNROLLS = (64, 32)
AHEAD = 3
BEHIND = 6
F32, BF16, I32 = jnp.float32, jnp.bfloat16, jnp.int32


def dot(a, b, contract=((1,), (0,))):
    return lax.dot_general(a, b, (contract, ((), ())), preferred_element_type=F32)


def tile_bits(n_local):
    return n_local.bit_length()


def iota(shape, axis):
    return lax.broadcasted_iota(I32, shape, axis)


def start_all(sems, *pairs):
    copies = [pltpu.make_async_copy(a, b, sems.at[k]) for k, (a, b) in enumerate(pairs)]
    for c in copies:
        c.start()
    return copies


def sort_kernel(
    n_col, share, live_ref, vol_hbm, slot_hbm, wanted_hbm, *refs
):
    inputs, (msg_ref, *copies_of) = refs[:3], refs[3:7]
    vol_ref, slot_ref, wanted_ref, sems, far_sems = refs[7:]
    near = start_all(sems, (vol_hbm, vol_ref), (slot_hbm, slot_ref), (wanted_hbm, wanted_ref))
    far = start_all(far_sems, *zip(inputs, copies_of))
    for c in near:
        c.wait()
    rows = vol_ref.shape[0]
    req = wanted_ref.shape[2]
    slot = slot_ref[...]
    vol = vol_ref[...].astype(F32)
    position = iota((rows, TILE), 0) * TILE + iota((rows, TILE), 1)
    peer, place = slot // req, slot % req
    key = 2 * peer + (vol_ref[...] // share == peer).astype(I32)
    key = jnp.where(position < live_ref[0], key, 2 * n_col)
    keys = 2 * n_col + 2
    masks = [(key == k).astype(F32) for k in range(keys)]
    mask = jnp.concatenate(masks, 0).astype(BF16)
    ahead = (iota((TILE, TILE), 0) < iota((TILE, TILE), 1)).astype(F32).astype(BF16)
    within = dot(mask, ahead)
    count = dot(mask, jnp.ones((TILE, TILE), BF16)).astype(BF16)
    total = keys * rows
    above = (iota((total, total), 1) < iota((total, total), 0)).astype(F32).astype(BF16)
    start = dot(above, count)
    rank = within + start
    dest = masks[0] * rank[:rows]
    for k in range(1, keys):
        dest += masks[k] * rank[k * rows : (k + 1) * rows]
    dest = dest.astype(I32)
    dest_row, dest_lane = dest // TILE, dest % TILE
    table = wanted_ref[0].astype(F32)
    if n_col % 8:
        table = jnp.concatenate([table, jnp.zeros((8 - n_col % 8, req), F32)], 0)
    table = table.astype(BF16)
    out = jnp.zeros((2 * rows, TILE), F32)
    for r in range(rows):
        row = slice(r, r + 1)
        chosen = (iota((req, TILE), 0) == place[row]).astype(F32).astype(BF16)
        tiles = dot(table, chosen)
        tiles = jnp.where(iota(tiles.shape, 0) == peer[row], tiles, 0.0)
        tile = jnp.sum(tiles, 0, keepdims=True)
        here = (iota((rows, TILE), 0) == dest_row[row]).astype(F32)
        values = jnp.concatenate([here * vol[row], here * tile], 0).astype(BF16)
        lanes = (iota((TILE, TILE), 0) == dest_lane[row]).astype(F32).astype(BF16)
        out += dot(values, lanes, ((1,), (1,)))
    msg_ref[: 2 * rows] = out.astype(I32)
    even, odd = (
        jnp.concatenate([start[k * rows : k * rows + 1] for k in range(first, keys, 2)], 0)
        for first in (0, 1)
    )
    tail = jnp.where(iota(even.shape, 1) < TILE // 2, even, odd)
    pad = msg_ref.shape[0] - 2 * rows - keys // 2
    if pad:
        tail = jnp.concatenate([tail, jnp.zeros((pad, TILE), F32)], 0)
    msg_ref[2 * rows :] = tail.astype(I32)
    for c in far:
        c.wait()


def thirds(a):
    one = a.astype(BF16).astype(F32)
    two = (a - one).astype(BF16).astype(F32)
    return one, two, a - one - two


def point_features(points):
    a = (points - 0.5) * (1.0 / RADIUS)
    norm = a[0:1] * a[0:1] + a[1:2] * a[1:2] + a[2:3] * a[2:3]
    return thirds(a), jnp.concatenate(thirds(norm), 0)


def feature_kernel(vol_ref, pts_ref, coef_ref, surf, vols, coefs):
    n_local, group_tiles = surf.shape[0] - 1, vols.shape[0]
    step = min(32, n_local, group_tiles)
    ones = jnp.ones((3, step * TILE), F32)
    blank = jnp.zeros((FEATS - 24, step * TILE), F32)

    def surface(b, _):
        lanes = pl.ds(pl.multiple_of(b * step * TILE, step * TILE), step * TILE)
        (one, two, three), norm = point_features(pts_ref[:, lanes])
        one, two, three = -2.0 * one, -2.0 * two, -2.0 * three
        rows = jnp.concatenate([one, two, one, three, one, two, norm, ones, blank], 0).astype(BF16)
        coef = coef_ref[:, lanes] * 4.0
        high = coef.astype(BF16).astype(F32)
        pair = jnp.concatenate([high, coef - high, jnp.zeros((2, step * TILE), F32)], 0)
        for t in range(step):
            span = slice(t * TILE, (t + 1) * TILE)
            surf[b * step + t] = rows[:, span].T
            tile = pair[:, span].astype(BF16)
            coefs[b * step + t] = jnp.concatenate([tile, tile], 1)
        return 0

    surf[n_local] = jnp.zeros((TILE, FEATS), BF16)
    coefs[n_local] = jnp.zeros((8, 2 * TILE), BF16)

    def volume(b, _):
        lanes = pl.ds(pl.multiple_of(b * step * TILE, step * TILE), step * TILE)
        (one, two, three), norm = point_features(vol_ref[:, lanes])
        rows = jnp.concatenate([one, one, two, one, three, two, ones, norm, blank], 0).astype(BF16)
        for t in range(step):
            vols[b * step + t] = rows[:, t * TILE : (t + 1) * TILE]
        return 0

    lax.fori_loop(0, group_tiles // step, volume, 0)
    lax.fori_loop(0, n_local // step, surface, 0)


def main_kernel(n_col, n_local, rows, own, me_ref, *refs):
    msgs = refs[:n_col]
    surf, vols, coefs = refs[n_col : n_col + 3]
    targets = [0] if own else range(n_col)
    outs = refs[n_col + 3 :][: len(targets)]
    packed, lists, past, now, acc, dist, kern, sem = refs[n_col + 3 + len(targets) :]
    unroll = UNROLLS[own]
    group_tiles = vols.shape[0]
    bits = tile_bits(n_local)
    me = me_ref[0]
    for k, msg in enumerate(msgs):
        packed[k * rows : (k + 1) * rows] = (msg[:rows] << bits) | msg[rows : 2 * rows]
        at = n_col * rows + 2 * k
        packed[at : at + 2] = msg[pl.ds(2 * rows + me, 2)]
    copy = pltpu.make_async_copy(packed, lists, sem)
    copy.start()
    acc[...] = jnp.zeros_like(acc)
    kern[unroll - BEHIND :] = jnp.zeros((BEHIND, 2 * TILE, TILE), BF16)
    copy.wait()
    bounds = []
    for k in range(n_col):
        at = n_col * rows + 2 * k
        bounds.append((lists[at, 0], lists[at, TILE // 2], lists[at + 1, 0]))
    ends, shifts = [], []
    total = jnp.int32(0)
    for part in range(2):
        for k in range(n_col):
            first, last = bounds[k][part], bounds[k][part + 1]
            shifts.append(k * rows * TILE + first - total)
            total = total + (last - first)
            ends.append(total)
    whole = (ends[n_col - 1] + UNROLLS[0] - 1) // UNROLLS[0]
    begin = whole * UNROLLS[0] if own else 0
    trips = jnp.maximum(total - begin + unroll - 1, 0) // unroll if own else whole

    def fetch(p):
        shift = shifts[own * n_col]
        for k in range(own * n_col + 1, 2 * n_col):
            shift = jnp.where(p >= ends[k - 1], shifts[k], shift)
        valid = p < total
        at = jnp.where(valid, p + shift, 0)
        return jnp.where(valid, lists[at >> 7, at & (TILE - 1)], n_local)

    def parts(pair):
        return pair >> bits, pair & ((1 << bits) - 1)

    def move(pair, q):
        v, s = parts(pair)
        acc[v] += dot(coefs[s], kern[q])

    def distance(pair):
        v, s = parts(pair)
        return dot(surf[s], vols[v])

    def evaluate(squared, q):
        squared = jnp.minimum(jnp.maximum(squared, 1e-12), 1.0)
        radius = squared * lax.rsqrt(squared)
        falloff = 1.0 - radius
        falloff = falloff * falloff
        value = falloff * falloff * (radius + 0.25)
        high = value.astype(BF16)
        kern[q, :TILE] = high
        kern[q, TILE:] = (value - high.astype(F32)).astype(BF16)

    for q in range(unroll):
        now[q] = fetch(jnp.int32(begin + q))
    for q in range(BEHIND):
        past[q] = n_local
    for q in range(AHEAD):
        dist[q] = distance(now[q])

    def trip(h, _):
        pairs = []
        squared = [dist[q] for q in range(AHEAD)]
        for q in range(unroll):
            pairs.append(now[q])
            now[q] = fetch(begin + (h + 1) * unroll + q)
            ahead = distance(now[(q + AHEAD) % unroll])
            if q + AHEAD < unroll:
                squared.append(ahead)
            else:
                dist[q + AHEAD - unroll] = ahead
            move(pairs[q - BEHIND] if q >= BEHIND else past[q], (q - BEHIND) % unroll)
            evaluate(squared[q], q)
        for q in range(BEHIND):
            past[q] = pairs[unroll - BEHIND + q]
        return 0

    lax.fori_loop(0, trips, trip, 0)
    for q in range(BEHIND):
        move(past[q], unroll - BEHIND + q)

    share = group_tiles // n_col
    for out, k in zip(outs, targets):
        base = lax.rem(me + k, n_col) * share
        for t in range(share):
            value = acc[base + t]
            out[:, t * TILE : (t + 1) * TILE] = value[:3] + value[3:6]


def shift_right(x, k, n):
    return lax.ppermute(x, "col", [(i, (i + k) % n) for i in range(n)])


def per_device(vol_pts, surf_pts, surf_coef, vol_tile, slot, wanted, live):
    n_col = lax.axis_size("col")
    me = lax.axis_index("col").astype(I32).reshape(1)
    n_local = surf_pts.shape[1] // TILE
    group_tiles = vol_pts.shape[1] // TILE
    share = group_tiles // n_col
    list_rows = vol_tile.shape[1] // TILE
    msg_rows = -(-(2 * list_rows + n_col + 1) // 8) * 8
    packed_rows = -(-(n_col * list_rows + 2 * n_col) // 8) * 8
    smem = pl.BlockSpec(memory_space=pltpu.SMEM)
    vmem = pl.BlockSpec(memory_space=pltpu.VMEM)
    hbm = pl.BlockSpec(memory_space=pltpu.HBM)

    def stay(x):
        return pltpu.with_memory_space_constraint(x, pltpu.HBM)

    inputs = (vol_pts, surf_pts, surf_coef)
    msg, *near = pl.pallas_call(
        functools.partial(sort_kernel, n_col, share),
        out_shape=[jax.ShapeDtypeStruct((msg_rows, TILE), I32)]
        + [jax.ShapeDtypeStruct(x.shape, x.dtype) for x in inputs],
        in_specs=[smem] + [hbm] * 6,
        out_specs=[vmem] * 4,
        scratch_shapes=[
            pltpu.VMEM((list_rows, TILE), I32),
            pltpu.VMEM((list_rows, TILE), I32),
            pltpu.VMEM(wanted.shape, I32),
            pltpu.SemaphoreType.DMA((3,)),
            pltpu.SemaphoreType.DMA((3,)),
        ],
        compiler_params=pltpu.CompilerParams(vmem_limit_bytes=8 << 20),
        name="sort_pairs",
    )(live, *map(stay, (vol_tile.reshape(-1, TILE), slot.reshape(-1, TILE), wanted, *inputs)))
    msgs = [msg] + [shift_right(msg, k, n_col) for k in range(1, n_col)]
    features = pl.pallas_call(
        feature_kernel,
        out_shape=[
            jax.ShapeDtypeStruct((n_local + 1, TILE, FEATS), BF16),
            jax.ShapeDtypeStruct((group_tiles, FEATS, TILE), BF16),
            jax.ShapeDtypeStruct((n_local + 1, 8, 2 * TILE), BF16),
        ],
        in_specs=[vmem] * 3,
        out_specs=[vmem] * 3,
        compiler_params=pltpu.CompilerParams(vmem_limit_bytes=16 << 20),
        name="features",
    )(*near)
    def sums(own, count):
        return pl.pallas_call(
            functools.partial(main_kernel, n_col, n_local, list_rows, own),
            out_shape=[jax.ShapeDtypeStruct((3, share * TILE), F32)] * count,
            in_specs=[smem] + [vmem] * (n_col + 3),
            out_specs=[vmem] * count,
            scratch_shapes=[
                pltpu.VMEM((packed_rows, TILE), I32),
                pltpu.SMEM((packed_rows, TILE), I32),
                pltpu.SMEM((BEHIND,), I32),
                pltpu.SMEM((UNROLLS[own],), I32),
                pltpu.VMEM((group_tiles, 8, TILE), F32),
                pltpu.VMEM((AHEAD, TILE, TILE), F32),
                pltpu.VMEM((UNROLLS[own], 2 * TILE, TILE), BF16),
                pltpu.SemaphoreType.DMA,
            ],
            compiler_params=pltpu.CompilerParams(vmem_limit_bytes=16 << 20),
            name="pair_sums_own" if own else "pair_sums_sent",
        )(me, *msgs, *features)

    out, *sent = sums(0, n_col)
    sent = [shift_right(x, k, n_col) for k, x in enumerate(sent, 1)]
    for x in (*sums(1, 1), *sent):
        out = out + x
    return out


def solution(mesh):
    return jax.shard_map(
        per_device,
        mesh=mesh,
        in_specs=(
            P(None, ("gx", "gy")),
            P(None, "col"),
            P(None, "col"),
            P(("gx", "gy", "col"), None),
            P(("gx", "gy", "col"), None),
            P(("gx", "gy", "col"), None, None),
            P(("gx", "gy", "col")),
        ),
        out_specs=P(None, ("gx", "gy", "col")),
        check_vma=False,
    )
```

```python
import functools

import jax
import jax.numpy as jnp
from jax import lax
from jax.experimental import pallas as pl
from jax.experimental.pallas import tpu as pltpu
from jax.sharding import PartitionSpec as P

TILE = 128
RADIUS = 1.2
FEATS = 32
UNROLLS = (64, 32)
KEPT = 128
AHEAD = 3
BEHIND = 6
F32, BF16, I32 = jnp.float32, jnp.bfloat16, jnp.int32


def dot(a, b, contract=((1,), (0,))):
    return lax.dot_general(a, b, (contract, ((), ())), preferred_element_type=F32)


def tile_bits(n_local):
    return n_local.bit_length()


def iota(shape, axis):
    return lax.broadcasted_iota(I32, shape, axis)


def start_all(sems, *pairs):
    copies = [pltpu.make_async_copy(a, b, sems.at[k]) for k, (a, b) in enumerate(pairs)]
    for c in copies:
        c.start()
    return copies


def sort_kernel(
    n_col, share, live_ref, vol_hbm, slot_hbm, wanted_hbm, *refs
):
    inputs, (msg_ref, *copies_of) = refs[:3], refs[3:7]
    vol_ref, slot_ref, wanted_ref, sems, far_sems = refs[7:]
    near = start_all(sems, (vol_hbm, vol_ref), (slot_hbm, slot_ref), (wanted_hbm, wanted_ref))
    far = start_all(far_sems, *zip(inputs, copies_of))
    for c in near:
        c.wait()
    rows = vol_ref.shape[0]
    req = wanted_ref.shape[2]
    slot = slot_ref[...]
    vol = vol_ref[...].astype(F32)
    position = iota((rows, TILE), 0) * TILE + iota((rows, TILE), 1)
    peer, place = slot // req, slot % req
    key = 2 * peer + (vol_ref[...] // share == peer).astype(I32)
    key = jnp.where(position < live_ref[0], key, 2 * n_col)
    keys = 2 * n_col + 2
    masks = [(key == k).astype(F32) for k in range(keys)]
    mask = jnp.concatenate(masks, 0).astype(BF16)
    ahead = (iota((TILE, TILE), 0) < iota((TILE, TILE), 1)).astype(F32).astype(BF16)
    within = dot(mask, ahead)
    count = dot(mask, jnp.ones((TILE, TILE), BF16)).astype(BF16)
    total = keys * rows
    above = (iota((total, total), 1) < iota((total, total), 0)).astype(F32).astype(BF16)
    start = dot(above, count)
    rank = within + start
    dest = masks[0] * rank[:rows]
    for k in range(1, keys):
        dest += masks[k] * rank[k * rows : (k + 1) * rows]
    dest = dest.astype(I32)
    dest_row, dest_lane = dest // TILE, dest % TILE
    table = wanted_ref[0].astype(F32)
    if n_col % 8:
        table = jnp.concatenate([table, jnp.zeros((8 - n_col % 8, req), F32)], 0)
    table = table.astype(BF16)
    out = jnp.zeros((2 * rows, TILE), F32)
    for r in range(rows):
        row = slice(r, r + 1)
        chosen = (iota((req, TILE), 0) == place[row]).astype(F32).astype(BF16)
        tiles = dot(table, chosen)
        tiles = jnp.where(iota(tiles.shape, 0) == peer[row], tiles, 0.0)
        tile = jnp.sum(tiles, 0, keepdims=True)
        here = (iota((rows, TILE), 0) == dest_row[row]).astype(F32)
        values = jnp.concatenate([here * vol[row], here * tile], 0).astype(BF16)
        lanes = (iota((TILE, TILE), 0) == dest_lane[row]).astype(F32).astype(BF16)
        out += dot(values, lanes, ((1,), (1,)))
    msg_ref[: 2 * rows] = out.astype(I32)
    even, odd = (
        jnp.concatenate([start[k * rows : k * rows + 1] for k in range(first, keys, 2)], 0)
        for first in (0, 1)
    )
    tail = jnp.where(iota(even.shape, 1) < TILE // 2, even, odd)
    pad = msg_ref.shape[0] - 2 * rows - keys // 2
    if pad:
        tail = jnp.concatenate([tail, jnp.zeros((pad, TILE), F32)], 0)
    msg_ref[2 * rows :] = tail.astype(I32)
    for c in far:
        c.wait()


def thirds(a):
    one = a.astype(BF16).astype(F32)
    two = (a - one).astype(BF16).astype(F32)
    return one, two, a - one - two


def point_features(points):
    a = (points - 0.5) * (1.0 / RADIUS)
    norm = a[0:1] * a[0:1] + a[1:2] * a[1:2] + a[2:3] * a[2:3]
    return thirds(a), jnp.concatenate(thirds(norm), 0)


def steps(tiles, body):
    step = min(32, tiles)

    def one(b, _):
        body(b * step, pl.ds(pl.multiple_of(b * step * TILE, step * TILE), step * TILE), step)
        return 0

    lax.fori_loop(0, tiles // step, one, 0)


def pad_rows(step):
    return jnp.ones((3, step * TILE), F32), jnp.zeros((FEATS - 24, step * TILE), F32)


def feature_kernel(pts_ref, surf):
    n_local = surf.shape[0] - 1

    def surface(tile, lanes, step):
        ones, blank = pad_rows(step)
        (one, two, three), norm = point_features(pts_ref[:, lanes])
        one, two, three = -2.0 * one, -2.0 * two, -2.0 * three
        rows = jnp.concatenate([one, two, one, three, one, two, norm, ones, blank], 0).astype(BF16)
        for t in range(step):
            surf[tile + t] = rows[:, t * TILE : (t + 1) * TILE].T

    steps(n_local, surface)
    surf[n_local] = jnp.zeros((TILE, FEATS), BF16)


def fill_volumes(vol_ref, vols):
    def volume(tile, lanes, step):
        ones, blank = pad_rows(step)
        (one, two, three), norm = point_features(vol_ref[:, lanes])
        rows = jnp.concatenate([one, one, two, one, three, two, ones, norm, blank], 0).astype(BF16)
        for t in range(step):
            vols[tile + t] = rows[:, t * TILE : (t + 1) * TILE]

    steps(vols.shape[0], volume)


def fill_coefs(coef_ref, coefs):
    n_local = coefs.shape[0] - 1

    def rows(tile, lanes, step):
        coef = coef_ref[:, lanes] * 4.0
        high = coef.astype(BF16).astype(F32)
        pair = jnp.concatenate([high, coef - high, jnp.zeros((2, step * TILE), F32)], 0)
        for t in range(step):
            one = pair[:, t * TILE : (t + 1) * TILE].astype(BF16)
            coefs[tile + t] = jnp.concatenate([one, one], 1)

    steps(n_local, rows)
    coefs[n_local] = jnp.zeros((8, 2 * TILE), BF16)


def main_kernel(n_col, n_local, rows, own, me_ref, *refs):
    msgs = refs[:n_col]
    surf, vols, coefs = refs[n_col : n_col + 3]
    outs, scratch = refs[n_col + 3 : -8], refs[-8:]
    packed, lists, past, now, acc, dist, kern, sem = scratch
    targets = [0] if own else range(n_col)
    if not own:
        vol_ref, coef_ref = vols, coefs
        *outs, vols, coefs = outs
    unroll = UNROLLS[own]
    group_tiles = vols.shape[0]
    bits = tile_bits(n_local)
    me = me_ref[0]
    for k, msg in enumerate(msgs):
        packed[k * rows : (k + 1) * rows] = (msg[:rows] << bits) | msg[rows : 2 * rows]
        at = n_col * rows + 2 * k
        packed[at : at + 2] = msg[pl.ds(2 * rows + me, 2)]
    copy = pltpu.make_async_copy(packed, lists, sem)
    copy.start()
    if not own:
        fill_volumes(vol_ref, vols)
        fill_coefs(coef_ref, coefs)
    acc[...] = jnp.zeros_like(acc)
    kern[unroll - BEHIND :] = jnp.zeros((BEHIND, 2 * TILE, TILE), BF16)
    copy.wait()
    bounds = []
    for k in range(n_col):
        at = n_col * rows + 2 * k
        bounds.append((lists[at, 0], lists[at, TILE // 2], lists[at + 1, 0]))
    ends, shifts = [], []
    total = jnp.int32(0)
    for part in range(2):
        for k in range(n_col):
            first, last = bounds[k][part], bounds[k][part + 1]
            shifts.append(k * rows * TILE + first - total)
            total = total + (last - first)
            ends.append(total)
    early = jnp.maximum(ends[n_col - 1], total - KEPT)
    whole = (early + UNROLLS[0] - 1) // UNROLLS[0]
    begin = whole * UNROLLS[0] if own else 0
    trips = jnp.maximum(total - begin + unroll - 1, 0) // unroll if own else whole

    def fetch(p):
        shift = shifts[own * n_col]
        for k in range(own * n_col + 1, 2 * n_col):
            shift = jnp.where(p >= ends[k - 1], shifts[k], shift)
        valid = p < total
        at = jnp.where(valid, p + shift, 0)
        return jnp.where(valid, lists[at >> 7, at & (TILE - 1)], n_local)

    def parts(pair):
        return pair >> bits, pair & ((1 << bits) - 1)

    def move(pair, q):
        v, s = parts(pair)
        acc[v] += dot(coefs[s], kern[q])

    def distance(pair):
        v, s = parts(pair)
        return dot(surf[s], vols[v])

    def evaluate(squared, q):
        squared = jnp.minimum(jnp.maximum(squared, 1e-12), 1.0)
        radius = squared * lax.rsqrt(squared)
        falloff = 1.0 - radius
        falloff = falloff * falloff
        value = falloff * falloff * (radius + 0.25)
        high = value.astype(BF16)
        kern[q, :TILE] = high
        kern[q, TILE:] = (value - high.astype(F32)).astype(BF16)

    for q in range(unroll):
        now[q] = fetch(jnp.int32(begin + q))
    for q in range(BEHIND):
        past[q] = n_local
    for q in range(AHEAD):
        dist[q] = distance(now[q])

    def trip(h, _):
        pairs = []
        squared = [dist[q] for q in range(AHEAD)]
        for q in range(unroll):
            pairs.append(now[q])
            now[q] = fetch(begin + (h + 1) * unroll + q)
            ahead = distance(now[(q + AHEAD) % unroll])
            if q + AHEAD < unroll:
                squared.append(ahead)
            else:
                dist[q + AHEAD - unroll] = ahead
            move(pairs[q - BEHIND] if q >= BEHIND else past[q], (q - BEHIND) % unroll)
            evaluate(squared[q], q)
        for q in range(BEHIND):
            past[q] = pairs[unroll - BEHIND + q]
        return 0

    lax.fori_loop(0, trips, trip, 0)
    for q in range(BEHIND):
        move(past[q], unroll - BEHIND + q)

    share = group_tiles // n_col
    for out, k in zip(outs, targets):
        base = lax.rem(me + k, n_col) * share
        for t in range(share):
            value = acc[base + t]
            out[:, t * TILE : (t + 1) * TILE] = value[:3] + value[3:6]


def shift_right(x, k, n):
    return lax.ppermute(x, "col", [(i, (i + k) % n) for i in range(n)])


def per_device(vol_pts, surf_pts, surf_coef, vol_tile, slot, wanted, live):
    n_col = lax.axis_size("col")
    me = lax.axis_index("col").astype(I32).reshape(1)
    n_local = surf_pts.shape[1] // TILE
    group_tiles = vol_pts.shape[1] // TILE
    share = group_tiles // n_col
    list_rows = vol_tile.shape[1] // TILE
    msg_rows = -(-(2 * list_rows + n_col + 1) // 8) * 8
    packed_rows = -(-(n_col * list_rows + 2 * n_col) // 8) * 8
    smem = pl.BlockSpec(memory_space=pltpu.SMEM)
    vmem = pl.BlockSpec(memory_space=pltpu.VMEM)
    hbm = pl.BlockSpec(memory_space=pltpu.HBM)

    def stay(x):
        return pltpu.with_memory_space_constraint(x, pltpu.HBM)

    inputs = (vol_pts, surf_pts, surf_coef)
    msg, *near = pl.pallas_call(
        functools.partial(sort_kernel, n_col, share),
        out_shape=[jax.ShapeDtypeStruct((msg_rows, TILE), I32)]
        + [jax.ShapeDtypeStruct(x.shape, x.dtype) for x in inputs],
        in_specs=[smem] + [hbm] * 6,
        out_specs=[vmem] * 4,
        scratch_shapes=[
            pltpu.VMEM((list_rows, TILE), I32),
            pltpu.VMEM((list_rows, TILE), I32),
            pltpu.VMEM(wanted.shape, I32),
            pltpu.SemaphoreType.DMA((3,)),
            pltpu.SemaphoreType.DMA((3,)),
        ],
        compiler_params=pltpu.CompilerParams(vmem_limit_bytes=8 << 20),
        name="sort_pairs",
    )(live, *map(stay, (vol_tile.reshape(-1, TILE), slot.reshape(-1, TILE), wanted, *inputs)))
    msgs = [msg] + [shift_right(msg, k, n_col) for k in range(n_col - 1, 0, -1)]
    vol_near, pts_near, coef_near = near
    surf = pl.pallas_call(
        feature_kernel,
        out_shape=jax.ShapeDtypeStruct((n_local + 1, TILE, FEATS), BF16),
        in_specs=[vmem],
        out_specs=vmem,
        compiler_params=pltpu.CompilerParams(vmem_limit_bytes=16 << 20),
        name="features",
    )(pts_near)

    def sums(own, points, coefs, out_shape):
        return pl.pallas_call(
            functools.partial(main_kernel, n_col, n_local, list_rows, own),
            out_shape=out_shape,
            in_specs=[smem] + [vmem] * (n_col + 3),
            out_specs=[vmem] * len(out_shape),
            scratch_shapes=[
                pltpu.VMEM((packed_rows, TILE), I32),
                pltpu.SMEM((packed_rows, TILE), I32),
                pltpu.SMEM((BEHIND,), I32),
                pltpu.SMEM((UNROLLS[own],), I32),
                pltpu.VMEM((group_tiles, 8, TILE), F32),
                pltpu.VMEM((AHEAD, TILE, TILE), F32),
                pltpu.VMEM((UNROLLS[own], 2 * TILE, TILE), BF16),
                pltpu.SemaphoreType.DMA,
            ],
            compiler_params=pltpu.CompilerParams(vmem_limit_bytes=16 << 20),
            name="pair_sums_own" if own else "pair_sums_sent",
        )(me, *msgs, surf, points, coefs)

    part = jax.ShapeDtypeStruct((3, share * TILE), F32)
    rows = [
        jax.ShapeDtypeStruct((group_tiles, FEATS, TILE), BF16),
        jax.ShapeDtypeStruct((n_local + 1, 8, 2 * TILE), BF16),
    ]
    out, *sent, vols, coefs = sums(0, vol_near, coef_near, [part] * n_col + rows)
    sent = [shift_right(x, k, n_col) for k, x in enumerate(sent, 1)]
    for x in (*sums(1, vols, coefs, [part]), *sent):
        out = out + x
    return out


def solution(mesh):
    return jax.shard_map(
        per_device,
        mesh=mesh,
        in_specs=(
            P(None, ("gx", "gy")),
            P(None, "col"),
            P(None, "col"),
            P(("gx", "gy", "col"), None),
            P(("gx", "gy", "col"), None),
            P(("gx", "gy", "col"), None, None),
            P(("gx", "gy", "col")),
        ),
        out_specs=P(None, ("gx", "gy", "col")),
        check_vma=False,
    )
```

```python
import functools

import jax
import jax.numpy as jnp
from jax import lax
from jax.experimental import pallas as pl
from jax.experimental.pallas import tpu as pltpu
from jax.sharding import PartitionSpec as P

TILE = 128
RADIUS = 1.2
FEATS = 32
UNROLLS = (64, 64)
KEPT = 128
AHEAD = 3
BEHIND = 6
F32, BF16, I32 = jnp.float32, jnp.bfloat16, jnp.int32


def dot(a, b, contract=((1,), (0,))):
    return lax.dot_general(a, b, (contract, ((), ())), preferred_element_type=F32)


def tile_bits(n_local):
    return n_local.bit_length()


def iota(shape, axis):
    return lax.broadcasted_iota(I32, shape, axis)


def start_all(sems, *pairs):
    copies = [pltpu.make_async_copy(a, b, sems.at[k]) for k, (a, b) in enumerate(pairs)]
    for c in copies:
        c.start()
    return copies


def sort_kernel(
    n_col, share, live_ref, vol_hbm, slot_hbm, wanted_hbm, *refs
):
    inputs, (msg_ref, *copies_of) = refs[:3], refs[3:7]
    vol_ref, slot_ref, wanted_ref, sems, far_sems = refs[7:]
    near = start_all(sems, (vol_hbm, vol_ref), (slot_hbm, slot_ref), (wanted_hbm, wanted_ref))
    far = start_all(far_sems, *zip(inputs, copies_of))
    for c in near:
        c.wait()
    rows = vol_ref.shape[0]
    req = wanted_ref.shape[2]
    slot = slot_ref[...]
    vol = vol_ref[...].astype(F32)
    position = iota((rows, TILE), 0) * TILE + iota((rows, TILE), 1)
    peer, place = slot // req, slot % req
    key = 2 * peer + (vol_ref[...] // share == peer).astype(I32)
    key = jnp.where(position < live_ref[0], key, 2 * n_col)
    keys = 2 * n_col + 2
    masks = [(key == k).astype(F32) for k in range(keys)]
    mask = jnp.concatenate(masks, 0).astype(BF16)
    ahead = (iota((TILE, TILE), 0) < iota((TILE, TILE), 1)).astype(F32).astype(BF16)
    within = dot(mask, ahead)
    count = dot(mask, jnp.ones((TILE, TILE), BF16)).astype(BF16)
    total = keys * rows
    above = (iota((total, total), 1) < iota((total, total), 0)).astype(F32).astype(BF16)
    start = dot(above, count)
    rank = within + start
    dest = masks[0] * rank[:rows]
    for k in range(1, keys):
        dest += masks[k] * rank[k * rows : (k + 1) * rows]
    dest = dest.astype(I32)
    dest_row, dest_lane = dest // TILE, dest % TILE
    table = wanted_ref[0].astype(F32)
    if n_col % 8:
        table = jnp.concatenate([table, jnp.zeros((8 - n_col % 8, req), F32)], 0)
    table = table.astype(BF16)
    out = jnp.zeros((2 * rows, TILE), F32)
    for r in range(rows):
        row = slice(r, r + 1)
        chosen = (iota((req, TILE), 0) == place[row]).astype(F32).astype(BF16)
        tiles = dot(table, chosen)
        tiles = jnp.where(iota(tiles.shape, 0) == peer[row], tiles, 0.0)
        tile = jnp.sum(tiles, 0, keepdims=True)
        here = (iota((rows, TILE), 0) == dest_row[row]).astype(F32)
        values = jnp.concatenate([here * vol[row], here * tile], 0).astype(BF16)
        lanes = (iota((TILE, TILE), 0) == dest_lane[row]).astype(F32).astype(BF16)
        out += dot(values, lanes, ((1,), (1,)))
    msg_ref[: 2 * rows] = out.astype(I32)
    even, odd = (
        jnp.concatenate([start[k * rows : k * rows + 1] for k in range(first, keys, 2)], 0)
        for first in (0, 1)
    )
    tail = jnp.where(iota(even.shape, 1) < TILE // 2, even, odd)
    pad = msg_ref.shape[0] - 2 * rows - keys // 2
    if pad:
        tail = jnp.concatenate([tail, jnp.zeros((pad, TILE), F32)], 0)
    msg_ref[2 * rows :] = tail.astype(I32)
    for c in far:
        c.wait()


def thirds(a):
    one = a.astype(BF16).astype(F32)
    two = (a - one).astype(BF16).astype(F32)
    return one, two, a - one - two


def point_features(points):
    a = (points - 0.5) * (1.0 / RADIUS)
    norm = a[0:1] * a[0:1] + a[1:2] * a[1:2] + a[2:3] * a[2:3]
    return thirds(a), jnp.concatenate(thirds(norm), 0)


def steps(tiles, body):
    step = min(32, tiles)

    def one(b, _):
        body(b * step, pl.ds(pl.multiple_of(b * step * TILE, step * TILE), step * TILE), step)
        return 0

    lax.fori_loop(0, tiles // step, one, 0)


def pad_rows(step):
    return jnp.ones((3, step * TILE), F32), jnp.zeros((FEATS - 24, step * TILE), F32)


def feature_kernel(pts_ref, surf):
    n_local = surf.shape[0] - 1

    def surface(tile, lanes, step):
        ones, blank = pad_rows(step)
        (one, two, three), norm = point_features(pts_ref[:, lanes])
        one, two, three = -2.0 * one, -2.0 * two, -2.0 * three
        rows = jnp.concatenate([one, two, one, three, one, two, norm, ones, blank], 0).astype(BF16)
        for t in range(step):
            surf[tile + t] = rows[:, t * TILE : (t + 1) * TILE].T

    steps(n_local, surface)
    surf[n_local] = jnp.zeros((TILE, FEATS), BF16)


def fill_volumes(vol_ref, vols):
    def volume(tile, lanes, step):
        ones, blank = pad_rows(step)
        (one, two, three), norm = point_features(vol_ref[:, lanes])
        rows = jnp.concatenate([one, one, two, one, three, two, ones, norm, blank], 0).astype(BF16)
        for t in range(step):
            vols[tile + t] = rows[:, t * TILE : (t + 1) * TILE]

    steps(vols.shape[0], volume)


def fill_coefs(coef_ref, coefs):
    n_local = coefs.shape[0] - 1

    def rows(tile, lanes, step):
        coef = coef_ref[:, lanes] * 4.0
        high = coef.astype(BF16).astype(F32)
        pair = jnp.concatenate([high, coef - high, jnp.zeros((2, step * TILE), F32)], 0)
        for t in range(step):
            one = pair[:, t * TILE : (t + 1) * TILE].astype(BF16)
            coefs[tile + t] = jnp.concatenate([one, one], 1)

    steps(n_local, rows)
    coefs[n_local] = jnp.zeros((8, 2 * TILE), BF16)


def main_kernel(n_col, n_local, rows, own, me_ref, *refs):
    msgs = refs[:n_col]
    surf, vols, coefs = refs[n_col : n_col + 3]
    outs, scratch = refs[n_col + 3 : -8], refs[-8:]
    packed, lists, past, now, acc, dist, kern, sem = scratch
    targets = [0] if own else range(n_col)
    if not own:
        vol_ref, coef_ref = vols, coefs
        *outs, vols, coefs = outs
    unroll = UNROLLS[own]
    group_tiles = vols.shape[0]
    bits = tile_bits(n_local)
    me = me_ref[0]
    for k, msg in enumerate(msgs):
        packed[k * rows : (k + 1) * rows] = (msg[:rows] << bits) | msg[rows : 2 * rows]
        at = n_col * rows + 2 * k
        packed[at : at + 2] = msg[pl.ds(2 * rows + me, 2)]
    copy = pltpu.make_async_copy(packed, lists, sem)
    copy.start()
    if not own:
        fill_volumes(vol_ref, vols)
        fill_coefs(coef_ref, coefs)
    acc[...] = jnp.zeros_like(acc)
    kern[unroll - BEHIND :] = jnp.zeros((BEHIND, 2 * TILE, TILE), BF16)
    copy.wait()
    bounds = []
    for k in range(n_col):
        at = n_col * rows + 2 * k
        bounds.append((lists[at, 0], lists[at, TILE // 2], lists[at + 1, 0]))
    ends, shifts = [], []
    total = jnp.int32(0)
    for part in range(2):
        for k in range(n_col):
            first, last = bounds[k][part], bounds[k][part + 1]
            shifts.append(k * rows * TILE + first - total)
            total = total + (last - first)
            ends.append(total)
    early = jnp.maximum(ends[n_col - 1], total - KEPT)
    whole = (early + UNROLLS[0] - 1) // UNROLLS[0]
    begin = whole * UNROLLS[0] if own else 0
    trips = jnp.maximum(total - begin + unroll - 1, 0) // unroll if own else whole

    def fetch(p):
        shift = shifts[own * n_col]
        for k in range(own * n_col + 1, 2 * n_col):
            shift = jnp.where(p >= ends[k - 1], shifts[k], shift)
        valid = p < total
        at = jnp.where(valid, p + shift, 0)
        return jnp.where(valid, lists[at >> 7, at & (TILE - 1)], n_local)

    def parts(pair):
        return pair >> bits, pair & ((1 << bits) - 1)

    def move(pair, q):
        v, s = parts(pair)
        acc[v] += dot(coefs[s], kern[q])

    def distance(pair):
        v, s = parts(pair)
        return dot(surf[s], vols[v])

    def evaluate(squared, q):
        squared = jnp.minimum(jnp.maximum(squared, 1e-12), 1.0)
        radius = squared * lax.rsqrt(squared)
        falloff = 1.0 - radius
        falloff = falloff * falloff
        value = falloff * falloff * (radius + 0.25)
        high = value.astype(BF16)
        kern[q, :TILE] = high
        kern[q, TILE:] = (value - high.astype(F32)).astype(BF16)

    for q in range(unroll):
        now[q] = fetch(jnp.int32(begin + q))
    for q in range(BEHIND):
        past[q] = n_local
    for q in range(AHEAD):
        dist[q] = distance(now[q])

    def trip(h, _):
        pairs = []
        squared = [dist[q] for q in range(AHEAD)]
        for q in range(unroll):
            pairs.append(now[q])
            now[q] = fetch(begin + (h + 1) * unroll + q)
            ahead = distance(now[(q + AHEAD) % unroll])
            if q + AHEAD < unroll:
                squared.append(ahead)
            else:
                dist[q + AHEAD - unroll] = ahead
            move(pairs[q - BEHIND] if q >= BEHIND else past[q], (q - BEHIND) % unroll)
            evaluate(squared[q], q)
        for q in range(BEHIND):
            past[q] = pairs[unroll - BEHIND + q]
        return 0

    lax.fori_loop(0, trips, trip, 0)
    for q in range(BEHIND):
        move(past[q], unroll - BEHIND + q)

    share = group_tiles // n_col
    for out, k in zip(outs, targets):
        base = lax.rem(me + k, n_col) * share
        for t in range(share):
            value = acc[base + t]
            out[:, t * TILE : (t + 1) * TILE] = value[:3] + value[3:6]


def shift_right(x, k, n):
    return lax.ppermute(x, "col", [(i, (i + k) % n) for i in range(n)])


def per_device(vol_pts, surf_pts, surf_coef, vol_tile, slot, wanted, live):
    n_col = lax.axis_size("col")
    me = lax.axis_index("col").astype(I32).reshape(1)
    n_local = surf_pts.shape[1] // TILE
    group_tiles = vol_pts.shape[1] // TILE
    share = group_tiles // n_col
    list_rows = vol_tile.shape[1] // TILE
    msg_rows = -(-(2 * list_rows + n_col + 1) // 8) * 8
    packed_rows = -(-(n_col * list_rows + 2 * n_col) // 8) * 8
    smem = pl.BlockSpec(memory_space=pltpu.SMEM)
    vmem = pl.BlockSpec(memory_space=pltpu.VMEM)
    hbm = pl.BlockSpec(memory_space=pltpu.HBM)

    def stay(x):
        return pltpu.with_memory_space_constraint(x, pltpu.HBM)

    inputs = (vol_pts, surf_pts, surf_coef)
    msg, *near = pl.pallas_call(
        functools.partial(sort_kernel, n_col, share),
        out_shape=[jax.ShapeDtypeStruct((msg_rows, TILE), I32)]
        + [jax.ShapeDtypeStruct(x.shape, x.dtype) for x in inputs],
        in_specs=[smem] + [hbm] * 6,
        out_specs=[vmem] * 4,
        scratch_shapes=[
            pltpu.VMEM((list_rows, TILE), I32),
            pltpu.VMEM((list_rows, TILE), I32),
            pltpu.VMEM(wanted.shape, I32),
            pltpu.SemaphoreType.DMA((3,)),
            pltpu.SemaphoreType.DMA((3,)),
        ],
        compiler_params=pltpu.CompilerParams(vmem_limit_bytes=8 << 20),
        name="sort_pairs",
    )(live, *map(stay, (vol_tile.reshape(-1, TILE), slot.reshape(-1, TILE), wanted, *inputs)))
    msgs = [msg] + [shift_right(msg, k, n_col) for k in range(n_col - 1, 0, -1)]
    vol_near, pts_near, coef_near = near
    surf = pl.pallas_call(
        feature_kernel,
        out_shape=jax.ShapeDtypeStruct((n_local + 1, TILE, FEATS), BF16),
        in_specs=[vmem],
        out_specs=vmem,
        compiler_params=pltpu.CompilerParams(vmem_limit_bytes=16 << 20),
        name="features",
    )(pts_near)

    def sums(own, points, coefs, out_shape):
        return pl.pallas_call(
            functools.partial(main_kernel, n_col, n_local, list_rows, own),
            out_shape=out_shape,
            in_specs=[smem] + [vmem] * (n_col + 3),
            out_specs=[vmem] * len(out_shape),
            scratch_shapes=[
                pltpu.VMEM((packed_rows, TILE), I32),
                pltpu.SMEM((packed_rows, TILE), I32),
                pltpu.SMEM((BEHIND,), I32),
                pltpu.SMEM((UNROLLS[own],), I32),
                pltpu.VMEM((group_tiles, 8, TILE), F32),
                pltpu.VMEM((AHEAD, TILE, TILE), F32),
                pltpu.VMEM((UNROLLS[own], 2 * TILE, TILE), BF16),
                pltpu.SemaphoreType.DMA,
            ],
            compiler_params=pltpu.CompilerParams(vmem_limit_bytes=16 << 20),
            name="pair_sums_own" if own else "pair_sums_sent",
        )(me, *msgs, surf, points, coefs)

    part = jax.ShapeDtypeStruct((3, share * TILE), F32)
    rows = [
        jax.ShapeDtypeStruct((group_tiles, FEATS, TILE), BF16),
        jax.ShapeDtypeStruct((n_local + 1, 8, 2 * TILE), BF16),
    ]
    out, *sent, vols, coefs = sums(0, vol_near, coef_near, [part] * n_col + rows)
    sent = [shift_right(x, k, n_col) for k, x in enumerate(sent, 1)]
    for x in (*sums(1, vols, coefs, [part]), *sent):
        out = out + x
    return out


def solution(mesh):
    return jax.shard_map(
        per_device,
        mesh=mesh,
        in_specs=(
            P(None, ("gx", "gy")),
            P(None, "col"),
            P(None, "col"),
            P(("gx", "gy", "col"), None),
            P(("gx", "gy", "col"), None),
            P(("gx", "gy", "col"), None, None),
            P(("gx", "gy", "col")),
        ),
        out_specs=P(None, ("gx", "gy", "col")),
        check_vma=False,
    )
```
